256 devices in a mesh: row: 32 (over x, y, core), col: 8 (over z).
Axes of the slice: x: 4, y: 4, z: 8, core: 2. Of those that a mesh axis runs over, the one named last changes fastest.
Arguments:
- kernel_tiles: float32 [32, 8, 9, 256, 512], P('row', 'col'), may hold values from -0.09375 to 0.09375
- footprints: int32 [32, 8, 9], P('row', 'col'), may hold values from 0 to 8, as said below
- counts: int32 [32, 8], P('row', 'col'), may hold values from 64 to 256, as said below
- readings: float32 [32, 8, 256], P('row', 'col'), may hold values from -6 to 6
- damping: float32 [1], replicated, may hold values from 0.1 to 0.5
- layer_depth: float32 [2], replicated, may hold values from 1 to 6
- inclinations: float32 [2], replicated, may hold values from 0.6 to 1.3
- declinations: float32 [2], replicated, may hold values from -3.140625 to 3.140625
- resid_grid: float32 [4096, 4096], P('col', 'row'), may hold values from -3 to 3
Outputs:
- coefficients: float32 [32, 8, 512], P('row', 'col')
- rtp_map: float32 [4096, 4096], P(('row', 'col'))
The draws below stay inside these ranges and needn't reach their ends.
Inputs may be any that keep to these rules, and one draw needn't show every extreme that they name: `footprints`: each tile's list holds each of the 9 codes once; code 3 (a + 1) + (b + 1) names the source block a tiles north and b tiles east of the tile; blocks outside the survey are empty. `counts`: reading slots from this count on are ignored.
All inputs are finite; a program needn't handle non-finite values.
Results may differ from the reference program's by a relative error of at most 0.0003.
Values sent between devices are 32-bit elements; how exact they have to be, the bound alone decides.
A program may use at most 128 MiB of HBM per device.

```python
import math
import jax
import jax.numpy as jnp
from jax import lax

READ_SLOTS = 256
SRC_ROWS = 8
SRC_COLS = 32
LAYERS = 2
REFINE = 16
FOOTPRINT = 9
CG_STEPS = 2
TILE_ROWS = 32
TILE_COLS = 8
BLOCK_SOURCES = 512
MAP_NORTH = 4096
MAP_EAST = 4096


def draw_footprints(key, part):
    tile_keys = jax.random.split(key, TILE_ROWS * TILE_COLS)
    orders = jax.vmap(lambda one_key: jax.random.permutation(one_key, FOOTPRINT))(tile_keys)
    return orders.reshape(TILE_ROWS, TILE_COLS, FOOTPRINT).astype(jnp.int32)


def draw_counts(key, part):
    values = jax.random.randint(key, (TILE_ROWS, TILE_COLS), READ_SLOTS // 4, READ_SLOTS + 1)
    return values.at[0, 0].set(READ_SLOTS).astype(jnp.int32)


def draw_readings(key, part):
    tiles_all = TILE_ROWS * TILE_COLS
    rising = 0.5 + jnp.arange(tiles_all, dtype=jnp.float32) / max(tiles_all - 1, 1)
    values = jnp.clip(jax.random.normal(jax.random.fold_in(key, 3), (tiles_all, READ_SLOTS)), -4.0, 4.0)
    return (rising[:, None] * values).reshape(TILE_ROWS, TILE_COLS, READ_SLOTS).astype(jnp.float32)


def block_scale(key, shape, cuts, least, top_value):
    gain = 1.0
    for dim, parts in cuts:
        heights = jax.random.uniform(jax.random.fold_in(jax.random.fold_in(key, 6), dim), (parts,), jnp.float32, least / len(cuts), top_value / len(cuts))
        gain = gain * jnp.repeat(jnp.exp(heights), shape[dim] // parts).reshape((-1,) + (1,) * (len(shape) - 1 - dim))
    return gain


def gaussian(key, dims, deviation, bound, shards=(), kind=jnp.bfloat16):
    loudness = block_scale(key, dims, shards, -0.22, 0.18) if shards else 1.0
    array = jax.random.normal(key, dims, jnp.float32) * deviation * loudness
    return jnp.minimum(jnp.maximum(array, -bound), bound).astype(kind)


def setup_inputs(seed: int = 0) -> dict:
    streams_of = jax.random.split(jax.random.key(seed), 10)
    return {
        "kernel_tiles": gaussian(streams_of[0], (TILE_ROWS, TILE_COLS, FOOTPRINT, READ_SLOTS, BLOCK_SOURCES), (FOOTPRINT * BLOCK_SOURCES) ** -0.5, 0.09375, ((0, 32), (1, 8)), jnp.float32),
        "footprints": draw_footprints(jax.random.fold_in(streams_of[9], 71), 0),
        "counts": draw_counts(jax.random.fold_in(streams_of[9], 71), 0),
        "readings": draw_readings(jax.random.fold_in(streams_of[9], 71), 0),
        "damping": jnp.clip(jnp.exp(jax.random.uniform(streams_of[4], (1,), jnp.float32, math.log(0.1), math.log(0.5))), 0.1, 0.5),
        "layer_depth": jnp.clip(jnp.exp(jax.random.uniform(streams_of[5], (LAYERS,), jnp.float32, math.log(1.0), math.log(6.0))), 1.0, 6.0),
        "inclinations": jnp.clip(jax.random.uniform(streams_of[6], (2,), jnp.float32, 0.6, 1.3), 0.6, 1.3),
        "declinations": jnp.clip(jax.random.uniform(streams_of[7], (2,), jnp.float32, -3.140625, 3.140625), -3.140625, 3.140625),
        "resid_grid": gaussian(streams_of[8], (MAP_EAST, MAP_NORTH), 0.5, 3.0, ((0, 8), (1, 32)), jnp.float32),
    }


HIGHEST_PRECISION = lax.Precision.HIGHEST
NEIGHBOUR_OFFSETS = tuple(((north_step, east_step) for north_step in (-1, 0, 1) for east_step in (-1, 0, 1)))

def hat_table(fine_start, fine_count, coarse_start, coarse_count):
    fine_pos = jnp.arange(fine_count, dtype=jnp.float32) + fine_start
    coarse_pos = jnp.arange(coarse_count, dtype=jnp.float32) + coarse_start
    offset = (fine_pos[:, None] + 0.5) / REFINE - 0.5 - coarse_pos[None, :]
    return jnp.maximum(0.0, 1.0 - jnp.abs(offset))

def frequency_of(positions, full_len):
    signed = jnp.where(positions < full_len // 2, positions, positions - full_len)
    return signed.astype(jnp.float32) / full_len

def pole_filter(north_freq, east_freq, inclinations, declinations):
    radius = jnp.sqrt(north_freq * north_freq + east_freq * east_freq)
    safe_radius = jnp.where(radius > 0.0, radius, 1.0)
    unit_north = jnp.where(radius > 0.0, north_freq / safe_radius, 0.0)
    unit_east = jnp.where(radius > 0.0, east_freq / safe_radius, 0.0)
    real_part = jnp.ones_like(radius)
    imag_part = jnp.zeros_like(radius)
    for member in range(2):
        vertical = jnp.sin(inclinations[member])
        horizontal = jnp.cos(inclinations[member])
        along_axis = horizontal * (jnp.cos(declinations[member]) * unit_north + jnp.sin(declinations[member]) * unit_east)
        denominator = vertical * vertical + along_axis * along_axis
        inv_real = vertical / denominator
        inv_imag = -along_axis / denominator
        real_part, imag_part = (real_part * inv_real - imag_part * inv_imag, real_part * inv_imag + imag_part * inv_real)
    return (real_part, imag_part)

def reference(kernel_tiles, footprints, counts, readings, damping, layer_depth, inclinations, declinations, resid_grid):
    live_mask = (jnp.arange(READ_SLOTS, dtype=jnp.int32)[None, None, :] < counts[:, :, None]).astype(jnp.float32)
    selector = (footprints[:, :, :, None] == jnp.arange(FOOTPRINT, dtype=jnp.int32)[None, None, None, :]).astype(jnp.float32)
    ridge_weight = damping[0]

    def forward(coefs_all):
        padded = jnp.pad(coefs_all, ((1, 1), (1, 1), (0, 0)))
        blocks = jnp.stack([padded[1 + north_step:1 + north_step + TILE_ROWS, 1 + east_step:1 + east_step + TILE_COLS] for north_step, east_step in NEIGHBOUR_OFFSETS], axis=2)
        chosen = jnp.einsum('abkc,abcs->abks', selector, blocks, precision=HIGHEST_PRECISION)
        return live_mask * jnp.einsum('abkrs,abks->abr', kernel_tiles, chosen, precision=HIGHEST_PRECISION)

    def adjoint(values):
        partial_sums = jnp.einsum('abkrs,abr->abks', kernel_tiles, live_mask * values, precision=HIGHEST_PRECISION)
        spread = jnp.einsum('abkc,abks->abcs', selector, partial_sums, precision=HIGHEST_PRECISION)
        summed = jnp.zeros((TILE_ROWS + 2, TILE_COLS + 2, BLOCK_SOURCES), jnp.float32)
        for position, (north_step, east_step) in enumerate(NEIGHBOUR_OFFSETS):
            summed = summed.at[1 + north_step:1 + north_step + TILE_ROWS, 1 + east_step:1 + east_step + TILE_COLS].add(spread[:, :, position])
        return summed[1:-1, 1:-1]

    def operate(vector):
        return adjoint(forward(vector)) + ridge_weight * vector
    right_side = adjoint(readings)
    solution = jnp.zeros_like(right_side)
    residual = right_side
    direction = right_side
    norm_now = jnp.sum(residual * residual)
    for iteration in range(CG_STEPS):
        applied = operate(direction)
        step_size = norm_now / jnp.sum(direction * applied)
        solution = solution + step_size * direction
        residual = residual - step_size * applied
        if iteration + 1 < CG_STEPS:
            norm_next = jnp.sum(residual * residual)
            direction = residual + norm_next / norm_now * direction
            norm_now = norm_next
    coarse = solution.reshape(TILE_ROWS, TILE_COLS, LAYERS, SRC_ROWS, SRC_COLS).transpose(2, 0, 3, 1, 4)
    coarse = coarse.reshape(LAYERS, TILE_ROWS * SRC_ROWS, TILE_COLS * SRC_COLS)
    up_north = hat_table(0.0, MAP_NORTH, 0.0, TILE_ROWS * SRC_ROWS)
    up_east = hat_table(0.0, MAP_EAST, 0.0, TILE_COLS * SRC_COLS)
    north_freq = frequency_of(jnp.arange(MAP_NORTH, dtype=jnp.int32), MAP_NORTH)[None, :]
    east_freq = frequency_of(jnp.arange(MAP_EAST, dtype=jnp.int32), MAP_EAST)[:, None]
    wavenumber = 2.0 * math.pi * jnp.sqrt(north_freq * north_freq + east_freq * east_freq)
    spectrum = jnp.fft.fft2(resid_grid)
    for layer in range(LAYERS):
        eastward = jnp.dot(up_east, coarse[layer].T, precision=HIGHEST_PRECISION)
        plane = jnp.dot(eastward, up_north.T, precision=HIGHEST_PRECISION)
        spectrum = spectrum + jnp.exp(-wavenumber * layer_depth[layer]) * jnp.fft.fft2(plane)
    row_block = MAP_EAST // TILE_COLS
    spec_blocks = spectrum.reshape(TILE_COLS, row_block, MAP_NORTH)
    east_blocks = east_freq.reshape(TILE_COLS, row_block, 1)

    def apply_filter(pair):
        spec_rows, east_rows = pair
        filt_real, filt_imag = pole_filter(north_freq, east_rows, inclinations, declinations)
        return spec_rows * (filt_real + 1j * filt_imag)
    filtered = lax.map(apply_filter, (spec_blocks, east_blocks)).reshape(MAP_EAST, MAP_NORTH)
    rtp_map = jnp.real(jnp.fft.ifft2(filtered)).astype(jnp.float32)
    return (solution, rtp_map)
```

```python
import functools
import math

import jax
import jax.numpy as jnp
import ml_dtypes
import numpy as np
from jax import lax
from jax.experimental import pallas as pl
from jax.experimental.pallas import tpu as pltpu
from jax.sharding import PartitionSpec as P

F32 = jnp.float32
BF16 = jnp.bfloat16
MESH = pl.DeviceIdType.MESH
ROWS, COLS = 32, 8
FULL = 4096
REFINE = 16
SLOTS = 256
OFFSETS = tuple((a, b) for a in (-1, 0, 1) for b in (-1, 0, 1))
SCALE = 1.0 / 16777216.0

(T1, T2A, T2B, TWIN, T3P, T3Q, ZP, RP, ZQ, RQ, Z1, R1, Z2, R2) = range(14)
PHASES = 14
RETURN0, COLLECT0, RETURN1, COLLECT1 = range(4)


def halves(x):
    high = x.astype(np.float32).astype(ml_dtypes.bfloat16)
    low = (x - high.astype(np.float64)).astype(np.float32).astype(ml_dtypes.bfloat16)
    return np.stack([high, low])


@functools.lru_cache(maxsize=None)
def tables():
    two_pi = 2.0 * math.pi
    a = np.arange(32)
    ka = np.arange(16)
    n = np.arange(128)
    kn = np.arange(128)
    ang_a = two_pi * np.outer(ka, a) / 32
    outer = np.stack([np.cos(ang_a), -np.sin(ang_a)])
    outer[1, 0] = (-1.0) ** a
    eye = np.eye(16)
    outer_fwd = np.kron(outer.reshape(32, 32), eye)
    inv = np.stack([2 * np.cos(ang_a), -2 * np.sin(ang_a)])
    inv[0, 0] = 1.0
    inv[1, 0] = (-1.0) ** a
    outer_inv = np.kron(inv.reshape(32, 32).T, eye)
    ang_t = two_pi * np.outer(ka, n) / 4096
    twist = np.stack([np.cos(ang_t), np.sin(ang_t)])[:, :, None, :]
    th = two_pi * np.outer(n, kn) / 128
    c, s = np.cos(th), np.sin(th)
    inner_fwd = np.block([[c, -s], [s, c]])
    inner_inv = np.block([[c, s], [-s, c]]).T
    inner_inv = np.block([[c.T, s.T], [-s.T, c.T]])
    k0 = np.arange(64)
    th0 = two_pi * np.outer(n, 32 * k0) / 4096
    th1 = two_pi * np.outer(n, 16 + 32 * k0) / 4096
    alt = (-1.0) ** n
    first_fwd = np.zeros((256, 256))
    first_fwd[:128, 0:64] = np.cos(th0)
    first_fwd[:128, 128:192] = -np.sin(th0)
    first_fwd[:128, 128] = alt
    first_fwd[128:, 64:128] = np.cos(th1)
    first_fwd[128:, 192:256] = -np.sin(th1)
    first_inv = np.zeros((256, 256))
    first_inv[0:64, :128] = 2 * np.cos(th0).T
    first_inv[0, :128] = 1.0
    first_inv[128:192, :128] = -2 * np.sin(th0).T
    first_inv[128, :128] = alt
    first_inv[64:128, 128:] = 2 * np.cos(th1).T
    first_inv[192:256, 128:] = -2 * np.sin(th1).T
    w = np.arange(512)
    th_w = two_pi * (np.outer(w, w) % 512) / 512
    east = np.concatenate([np.cos(th_w), np.sin(th_w)])
    kb = np.arange(8)
    ang_c = two_pi * np.outer(np.arange(32), 16 * kb) / 4096
    twist_coarse = np.concatenate([np.cos(ang_c), np.sin(ang_c)], axis=1)
    ang_f = two_pi * np.outer(kb, np.arange(16)) / 4096
    twist_fine = np.broadcast_to(
        np.stack([np.cos(ang_f), np.sin(ang_f)])[..., None], (2, 8, 16, 128)
    )
    u = np.arange(4096)
    g = np.arange(256)
    hat = np.maximum(0.0, 1.0 - np.abs((u[:, None] + 0.5) / REFINE - 0.5 - g[None, :]))
    spec = np.fft.fft(hat, axis=0)
    east_hat = np.stack(
        [np.concatenate([spec[k::8].real, spec[k::8].imag]) for k in range(8)]
    )
    order = np.array(
        [8 * i + 4 * m2 + g4 for i in range(32) for g4 in range(4) for m2 in range(2)]
    )
    north_hat = np.zeros((32, 144, 256))
    lane = np.arange(64)
    for col in range(8):
        for ka1 in range(2):
            for knh in range(2):
                slot = 2 * col + ka1
                ku = slot + 32 * (64 * knh + lane) if slot else 16 * knh + 32 * lane
                idx = col * 4 + ka1 * 2 + knh
                north_hat[idx, :64] = spec[ku].real[:, order]
                north_hat[idx, 64:128] = spec[ku].imag[:, order]
    north_hat[0, 128] = spec[2048].real[order]
    f32 = np.float32
    return dict(
        outer_fwd=halves(outer_fwd),
        outer_inv=halves(outer_inv),
        inner_fwd=halves(inner_fwd),
        inner_inv=halves(inner_inv),
        first_fwd=halves(first_fwd),
        first_inv=halves(first_inv),
        east=halves(east),
        twist=twist.astype(f32),
        twist_fine=np.ascontiguousarray(twist_fine).astype(f32),
        twist_coarse=twist_coarse.astype(f32),
        east_hat=np.ascontiguousarray(halves(east_hat).swapaxes(0, 1)),
        north_hat=np.ascontiguousarray(halves(north_hat).swapaxes(0, 1)),
    )


TABLE_NAMES = (
    "outer_fwd",
    "inner_fwd",
    "first_fwd",
    "twist",
    "twist_fine",
    "east",
    "north_hat",
    "east_hat",
    "inner_inv",
    "first_inv",
    "outer_inv",
)


def split(x):
    high = x.astype(BF16)
    return high, (x - high.astype(F32)).astype(BF16)


def dot3(lhs, rhs, transposed=False):
    dims = (((1,), (1 if transposed else 0,)), ((), ()))

    def one(x, y):
        return lax.dot_general(x, y, dims, preferred_element_type=F32)

    return one(lhs[0], rhs[0]) + (one(lhs[0], rhs[1]) + one(lhs[1], rhs[0]))


def short_transform(values, sign):
    count = len(values)
    if count == 1:
        return values
    even = short_transform(values[0::2], sign)
    odd = short_transform(values[1::2], sign)
    out = [None] * count
    for k in range(count // 2):
        re, im = odd[k]
        if k == 0:
            pass
        elif 4 * k == count:
            re, im = -sign * im, sign * re
        else:
            co = math.cos(2 * math.pi * k / count)
            si = sign * math.sin(2 * math.pi * k / count)
            re, im = re * co - im * si, re * si + im * co
        ere, eim = even[k]
        out[k] = (ere + re, eim + im)
        out[k + count // 2] = (ere - re, eim - im)
    return out


def pole_of(fn, fe, angles):
    radius = jnp.sqrt(fn * fn + fe * fe)
    safe = jnp.where(radius > 0.0, radius, 1.0)
    nn = jnp.where(radius > 0.0, fn / safe, 0.0)
    ne = jnp.where(radius > 0.0, fe / safe, 0.0)
    re = im = None
    for m in range(2):
        vertical = angles[m]
        horizontal = angles[2 + m]
        along = horizontal * (angles[4 + m] * nn + angles[6 + m] * ne)
        inverse = 1.0 / (vertical * vertical + along * along)
        one_re, one_im = vertical * inverse, -along * inverse
        if re is None:
            re, im = one_re, one_im
        else:
            re, im = re * one_re - im * one_im, re * one_im + im * one_re
    return re, im, radius


def lanes_of(shape):
    return lax.broadcasted_iota(jnp.int32, shape, len(shape) - 1)


def signs_of(shape):
    return jnp.where(lanes_of(shape) < 64, 1.0, -1.0).astype(F32)


def swap(x):
    return pltpu.roll(x, 64, axis=x.ndim - 1)


def kernel(
    foot, where_code, counts, params, twist_coarse,
    tiles_hbm, readings, grid,
    outer_fwd_h, inner_fwd_h, first_fwd_h, twist_h, twist_fine_h, east_h,
    north_hat_h, east_hat_h, inner_inv_h, first_inv_h, outer_inv_h,
    coef_out, map_out,
    tiles, outer_fwd, inner_fwd, first_fwd, twist, twist_fine, east,
    north_hat, east_hat, inner_inv, first_inv, outer_inv,
    in1, send2, in2, send3, in3, twin_send, twin_in, send4, in4, send5, in5,
    spec_main, spec_twin, filt,
    spread0, spread1, ret0, ret1, halo0, halo1, chosen,
    p_own, q_own, zp, zq, xp_send, xq_send, xp, xq,
    y_p, y_q, sum1, sum2, sum1b, sum2b, z1, r1, z2, r2,
    load_sem, send_sem, recv_sem, halo_send, halo_recv,
):
    r = lax.axis_index("row")
    c = lax.axis_index("col")
    kb = r // 4
    low2 = r % 4
    special = (c == 0) & (low2 == 0)

    loads = [
        (tiles_hbm, tiles),
        (outer_fwd_h, outer_fwd),
        (inner_fwd_h, inner_fwd),
        (first_fwd_h, first_fwd),
        (twist_h, twist),
        (twist_fine_h, twist_fine),
        (east_h, east),
        (north_hat_h.at[c * 4 + low2], north_hat),
        (east_hat_h.at[kb], east_hat),
        (inner_inv_h, inner_inv),
        (first_inv_h, first_inv),
        (outer_inv_h, outer_inv),
    ]
    copies = [
        pltpu.make_async_copy(src, dst, load_sem.at[i]) for i, (src, dst) in enumerate(loads)
    ]
    for one in copies:
        one.start()

    barrier = pltpu.get_barrier_semaphore()

    def greet(row, col):
        pl.semaphore_signal(barrier, inc=1, device_id=(row, col), device_id_type=MESH)

    def exists(a, b):
        return (r + a >= 0) & (r + a < ROWS) & (c + b >= 0) & (c + b < COLS)

    @pl.loop(1, ROWS)
    def _(i):
        greet((r + i) % ROWS, c)

    @pl.loop(1, COLS)
    def _(i):
        greet(r, (c + i) % COLS)

    expected = jnp.int32(ROWS - 1 + COLS - 1)
    for a in (-1, 1):
        for b in (-1, 1):
            there = exists(a, b)
            expected = expected + there.astype(jnp.int32)

            @pl.when(there)
            def _():
                greet(r + a, c + b)

    self_last = kb == c

    @pl.loop(0, COLS)
    def _(i):
        @pl.when(jnp.logical_not(self_last & (i == kb)))
        def _():
            greet(i * 4 + low2, kb)

        @pl.when(jnp.logical_not(self_last & (i == c)))
        def _():
            greet(c * 4 + low2, i)

    expected = expected + 16 - 2 * self_last.astype(jnp.int32)
    pl.semaphore_wait(barrier, expected)

    def push(src, dst, phase, row, col):
        pltpu.make_async_remote_copy(
            src_ref=src, dst_ref=dst, send_sem=send_sem.at[phase], recv_sem=recv_sem.at[phase],
            device_id=(row, col), device_id_type=MESH,
        ).start()

    def keep(src, dst, phase):
        pltpu.make_async_copy(src, dst, recv_sem.at[phase]).start()

    def arrived(dst, phase):
        pltpu.make_async_copy(dst, dst, recv_sem.at[phase]).wait()

    def left(ref, phase):
        pltpu.make_async_copy(ref, ref, send_sem.at[phase]).wait()

    def rows_exchange(src, dst, phase):
        keep(src.at[r], dst.at[r], phase)

        @pl.loop(1, ROWS)
        def _(i):
            row = (r + i) % ROWS
            push(src.at[row], dst.at[r], phase, row, c)

    def cols_exchange(src, dst, phase):
        keep(src.at[c], dst.at[c], phase)

        @pl.loop(1, COLS)
        def _(i):
            col = (c + i) % COLS
            push(src.at[col], dst.at[c], phase, r, col)

    def rows_share(src, dst, phase):
        keep(src, dst.at[r], phase)

        @pl.loop(1, ROWS)
        def _(i):
            push(src, dst.at[r], phase, (r + i) % ROWS, c)

    def cols_share(src, dst, phase):
        keep(src, dst.at[c], phase)

        @pl.loop(1, COLS)
        def _(i):
            push(src, dst.at[c], phase, r, (c + i) % COLS)

    def halo_copy(src, dst, turn, code, row, col):
        return pltpu.make_async_remote_copy(
            src_ref=src, dst_ref=dst,
            send_sem=halo_send.at[turn, code], recv_sem=halo_recv.at[turn, code],
            device_id=(row, col), device_id_type=MESH,
        )

    def return_start(spread, dst, turn):
        for code, (a, b) in enumerate(OFFSETS):
            if code != 4:

                @pl.when(exists(a, b))
                def _():
                    halo_copy(spread.at[code], dst.at[code], turn, code, r + a, c + b).start()

    def collect_start(own, dst, turn):
        for code, (a, b) in enumerate(OFFSETS):
            if code != 4:

                @pl.when(exists(-a, -b))
                def _():
                    halo_copy(own, dst.at[code], turn, code, r - a, c - b).start()

    def halo_wait(src, dst, turn, collecting):
        for code, (a, b) in enumerate(OFFSETS):
            if code != 4:
                away = -1 if collecting else 1
                source = exists(-away * a, -away * b)

                @pl.when(source)
                def _():
                    halo_copy(src, dst.at[code], turn, code, r, c).wait_recv()

                @pl.when(jnp.logical_not(source))
                def _():
                    dst[code] = jnp.zeros((8, 128), F32)

    def halo_left(src, dst, turn, collecting):
        for code, (a, b) in enumerate(OFFSETS):
            if code != 4:
                away = -1 if collecting else 1

                @pl.when(exists(away * a, away * b))
                def _():
                    halo_copy(src, dst.at[code], turn, code, r, c).wait_send()

    sub8 = lax.broadcasted_iota(jnp.int32, (8, 128), 0)

    def spread_of(y, out):
        @pl.loop(0, 9)
        def _(code):
            k = where_code[code]
            total = jnp.zeros((8, 128), F32)
            for m in range(4):
                acc = [jnp.zeros((8, 128), F32) for _ in range(4)]
                for t in range(32):
                    part = tiles[k, pl.ds(8 * t, 8), pl.ds(128 * m, 128)]
                    acc[t % 4] = acc[t % 4] + part * y[pl.ds(8 * t, 8), :]
                row = jnp.sum((acc[0] + acc[1]) + (acc[2] + acc[3]), axis=0, keepdims=True)
                total = total + jnp.where(sub8 == m, jnp.broadcast_to(row, (8, 128)), 0.0)
            out[code] = total

    def readings_of(blocks, y):
        @pl.loop(0, 8)
        def _(chunk):
            base = pl.multiple_of(32 * chunk, 32)
            acc = [jnp.zeros((8, 128), F32) for _ in range(4)]
            for k in range(9):
                code = foot[k]
                for m in range(4):
                    row = jnp.broadcast_to(blocks[code, pl.ds(m, 1), :], (8, 128))
                    for t in range(4):
                        part = tiles[k, pl.ds(base + 8 * t, 8), pl.ds(128 * m, 128)]
                        acc[t] = acc[t] + part * row
            for t in range(4):
                slot = lax.broadcasted_iota(jnp.int32, (8, 128), 0) + (base + 8 * t)
                total = jnp.sum(acc[t], axis=1, keepdims=True)
                y[pl.ds(base + 8 * t, 8), :] = jnp.where(
                    slot < counts[0], jnp.broadcast_to(total, (8, 128)), 0.0
                )

    def gather_blocks(own, halo):
        for code in range(9):
            chosen[code] = own[...] if code == 4 else halo[code]

    def own_sum(spread, ret):
        total = spread[4]
        for code in range(9):
            if code != 4:
                total = total + ret[code]
        return total

    def total_of(x):
        return jnp.sum(jnp.sum(x, axis=1, keepdims=True), axis=0, keepdims=True)

    lane8 = lanes_of((8, 128))

    def pack(parts):
        out = jnp.zeros((8, 128), F32)
        for i, part in enumerate(parts):
            out = out + jnp.where(
                (lane8 == i) & (sub8 == 0), jnp.broadcast_to(part, (8, 128)), 0.0
            )
        return out

    def unpack(x, i):
        return total_of(jnp.where((lane8 == i) & (sub8 == 0), x, 0.0))

    rows_exchange(grid, in1, T1)

    eye = lax.broadcasted_iota(jnp.int32, (SLOTS, SLOTS), 0) == lanes_of((SLOTS, SLOTS))
    column = jnp.sum(
        jnp.where(eye, jnp.broadcast_to(readings[...], (SLOTS, SLOTS)), 0.0),
        axis=1, keepdims=True,
    )
    slot_index = lax.broadcasted_iota(jnp.int32, (SLOTS, 128), 0)
    y_q[...] = jnp.where(slot_index < counts[0], jnp.broadcast_to(column, (SLOTS, 128)), 0.0)
    copies[0].wait()
    spread_of(y_q, spread0)
    return_start(spread0, ret0, RETURN0)

    for i in range(1, 6):
        copies[i].wait()
    arrived(in1, T1)
    outer = dot3(
        (outer_fwd[0], outer_fwd[1]), split(in1[...].reshape(512, 128))
    ).reshape(2, 16, 16, 128)
    tw_c, tw_s = twist[0], twist[1]
    turned = jnp.concatenate(
        [
            (outer[0] * tw_c + outer[1] * tw_s).reshape(256, 128),
            (outer[1] * tw_c - outer[0] * tw_s).reshape(256, 128),
        ],
        axis=1,
    )
    turned_h, turned_l = split(turned)
    send2[...] = dot3((turned_h, turned_l), (inner_fwd[0], inner_fwd[1])).reshape(8, 32, 256)
    send2[0, 0:16, :] = dot3((turned_h[:16], turned_l[:16]), (first_fwd[0], first_fwd[1]))
    cols_exchange(send2, in2, T2A)

    halo_wait(spread0.at[4], ret0, RETURN0, False)
    p_own[...] = own_sum(spread0, ret0)
    collect_start(p_own, halo0, COLLECT0)
    cols_share(p_own, zp, ZP)
    halo_wait(p_own, halo0, COLLECT0, True)
    gather_blocks(p_own, halo0)
    readings_of(chosen, y_p)
    p_val = p_own[...]
    sum1[...] = pack([total_of(y_p[...] * y_p[...]) * (1.0 / 128.0), total_of(p_val * p_val)])
    cols_share(sum1, z1, Z1)
    spread_of(y_p, spread1)
    return_start(spread1, ret1, RETURN1)

    lane_half = lanes_of((8, 128)) // 32

    def coarse_rows(z, out):
        for half in range(2):
            for g in range(4):
                total = jnp.zeros((8, 128), F32)
                for j in range(4):
                    block = z[4 * half + j]
                    shift = (32 * (j - g)) % 128
                    if shift:
                        block = pltpu.roll(block, shift, axis=1)
                    total = jnp.where(lane_half == j, block, total)
                lanes = pl.ds(128 * half, 128)
                out[pl.ds(2 * g, 2), lanes] = total[0:2]
                out[pl.ds(8 + 2 * g, 2), lanes] = total[2:4]

    arrived(zp, ZP)
    coarse_rows(zp, xp_send)
    rows_share(xp_send, xp, RP)

    arrived(in2, T2A)
    pairs = short_transform(
        [(in2[b, :, 0:128], in2[b, :, 128:256]) for b in range(8)], -1.0
    )
    lane32 = lanes_of((32, 128))
    sub32 = lax.broadcasted_iota(jnp.int32, (32, 128), 0)
    apart = (lane32 == 0) & (sub32 < 16) & (c == 0)
    left16 = lanes_of((16, 128)) < 64
    for k in range(8):
        re, im = pairs[k]
        other_re, other_im = pairs[(8 - k) % 8]
        main_re = jnp.where(apart, 0.5 * (re + other_re), re)
        main_im = jnp.where(apart, 0.5 * (im - other_im), im)
        twin_re = 0.5 * (im[:16] + other_im[:16])
        twin_im = 0.5 * (other_re[:16] - re[:16])
        co = twist_coarse[r, k]
        si = twist_coarse[r, 8 + k]
        fine_c, fine_s = twist_fine[0, k], twist_fine[1, k]
        tc = co * fine_c - si * fine_s
        ts = si * fine_c + co * fine_s
        for ka1 in range(2):
            xr, xi = main_re[16 * ka1:16 * ka1 + 16], main_im[16 * ka1:16 * ka1 + 16]
            yr, yi = xr * tc + xi * ts, xi * tc - xr * ts
            send3[4 * k + 2 * ka1] = jnp.where(left16, yr, swap(yi))
            send3[4 * k + 2 * ka1 + 1] = jnp.where(left16, swap(yr), yi)
        yr, yi = twin_re * tc + twin_im * ts, twin_im * tc - twin_re * ts
        twin_send[k] = jnp.where(left16, yr, swap(yi))
    rows_exchange(send3, in3, T2B)

    @pl.when(c == 0)
    def _():
        @pl.loop(0, 8)
        def _(k):
            @pl.when(4 * k == r)
            def _():
                keep(twin_send.at[k], twin_in.at[r], TWIN)

            @pl.when(4 * k != r)
            def _():
                push(twin_send.at[k], twin_in.at[r], TWIN, 4 * k, c)

    halo_wait(spread1.at[4], ret1, RETURN1, False)
    damping = params[0]
    q_own[...] = own_sum(spread1, ret1) + damping * p_own[...]
    collect_start(q_own, halo1, COLLECT1)
    cols_share(q_own, zq, ZQ)

    arrived(z1, Z1)
    half_sum = z1[0]
    for i in range(1, 8):
        half_sum = half_sum + z1[i]
    sum1b[...] = half_sum
    rows_share(sum1b, r1, R1)

    halo_wait(q_own, halo1, COLLECT1, True)
    gather_blocks(q_own, halo1)
    readings_of(chosen, y_q)

    arrived(zq, ZQ)
    coarse_rows(zq, xq_send)
    rows_share(xq_send, xq, RQ)

    arrived(r1, R1)
    full_sum = jnp.sum(r1[...], axis=0)
    g00, rr0 = unpack(full_sum, 0), unpack(full_sum, 1)
    step0 = rr0 / (g00 + damping * rr0)
    p_val = p_own[...]
    resid = p_val - step0 * q_own[...]
    yr1 = y_p[...] - step0 * y_q[...]
    sum2[...] = pack(
        [
            total_of(yr1 * yr1) * (1.0 / 128.0),
            total_of(yr1 * y_p[...]) * (1.0 / 128.0),
            total_of(resid * resid),
            total_of(resid * p_val),
        ]
    )
    cols_share(sum2, z2, Z2)

    knh = low2 % 2
    ka = 2 * c + low2 // 2

    @pl.loop(0, 16)
    def _(chunk):
        base = pl.multiple_of(32 * chunk, 32)
        shape = (32, 128)
        lane = lanes_of(shape)
        kv = kb + 8 * (lax.broadcasted_iota(jnp.int32, shape, 0) + base)
        ku = jnp.where(ka > 0, ka + 32 * (64 * knh + lane), 16 * knh + 32 * lane)
        ku = jnp.where(lane < 64, ku, 2048)
        fe = jnp.where(kv < 2048, kv, kv - 4096).astype(F32) * (1.0 / 4096.0)
        fn = jnp.where(ku < 2048, ku, ku - 4096).astype(F32) * (1.0 / 4096.0)
        angles = [params[3 + i] for i in range(8)]
        re_a, im_a, radius = pole_of(fn, fe, angles)
        re_b, im_b, _ = pole_of(
            jnp.where(ku == 2048, 0.5, fn), jnp.where(kv == 2048, 0.5, fe), angles
        )
        kappa = (2.0 * math.pi) * radius
        made = [
            (0.5 * SCALE) * (re_a + re_b),
            (0.5 * SCALE) * (im_a + im_b),
            jnp.exp(-kappa * params[1]),
            jnp.exp(-kappa * params[2]),
        ]
        for i, one in enumerate(made):
            other = swap(one)
            main = jnp.where(lane < 64, one, other)
            twin = jnp.where(lane < 64, other, one)
            if i == 1:
                sign = signs_of(shape)
                main, twin = main * sign, twin * sign
            filt[i, pl.ds(base, 32), :] = main
            filt[4 + i, pl.ds(base, 32), :] = twin

    copies[6].wait()
    arrived(in3, T2B)

    @pl.when(special)
    def _():
        arrived(twin_in, TWIN)

    @pl.when(jnp.logical_not(special))
    def _():
        twin_in[...] = jnp.zeros((32, 16, 128), F32)

    both = jnp.concatenate(
        [in3[...].reshape(512, 128), twin_in[...].reshape(512, 128)], axis=1
    )
    spun = dot3((east[0], east[1]), split(both))
    sign512 = signs_of((512, 128))
    spec_main[...] = spun[:512, :128] + sign512 * swap(spun[512:, :128])
    spec_twin[...] = spun[:512, 128:] + sign512 * swap(spun[512:, 128:])

    arrived(z2, Z2)
    half_sum = z2[0]
    for i in range(1, 8):
        half_sum = half_sum + z2[i]
    sum2b[...] = half_sum
    rows_share(sum2b, r2, R2)

    arrived(xp, RP)
    arrived(xq, RQ)
    for i in range(7, 12):
        copies[i].wait()
    arrived(r2, R2)
    full_sum = jnp.sum(r2[...], axis=0)
    g11, g10 = unpack(full_sum, 0), unpack(full_sum, 1)
    rr1, r10 = unpack(full_sum, 2), unpack(full_sum, 3)
    beta = rr1 / rr0
    bent = (g11 + 2.0 * beta * g10 + beta * beta * g00) + damping * (
        rr1 + 2.0 * beta * r10 + beta * beta * rr0
    )
    step1 = rr1 / bent
    coef_out[...] = step0 * p_val + step1 * (resid + beta * p_val)

    alpha = step0 + step1 + step1 * beta
    gamma = -step1 * step0
    rows_of = []
    extra = []
    for layer in range(2):
        coarse = alpha * xp[:, 8 * layer:8 * layer + 8, :].reshape(256, 256) + gamma * xq[
            :, 8 * layer:8 * layer + 8, :
        ].reshape(256, 256)
        north = dot3((north_hat[0], north_hat[1]), split(coarse))
        rows_of.append(north[:128])
        extra.append(north[128:144])
    rows_of.extend(extra)
    rows_of.append(jnp.zeros((96, 256), F32))
    model = dot3(
        (east_hat[0], east_hat[1]), split(jnp.concatenate(rows_of, axis=0)), transposed=True
    )
    left512 = lanes_of((512, 128)) < 64
    total = spec_main[...]
    twin = spec_twin[...]
    for layer in range(2):
        lanes = slice(128 * layer, 128 * layer + 128)
        plane = model[:512, lanes] - sign512 * swap(model[512:, lanes])
        total = total + filt[2 + layer] * plane
        top, bottom = model[:512, 256:], model[512:, 256:]
        if layer:
            top = pltpu.roll(top, 112, axis=1)
            bottom = pltpu.roll(bottom, 112, axis=1)
        twin = twin + filt[6 + layer] * jnp.where(left512, top, swap(bottom))
    shaped = filt[0] * total - filt[1] * swap(total)
    shaped_twin = filt[4] * twin - filt[5] * swap(twin)
    joined = special & (lanes_of((512, 128)) % 64 == 0)
    shaped = shaped - jnp.where(joined, sign512 * swap(shaped_twin), 0.0)

    spun = dot3((east[0], east[1]), split(shaped))
    back = spun[:512] - sign512 * swap(spun[512:])
    sign16 = signs_of((16, 128))
    fine_c, fine_s = twist_fine[0, kb], twist_fine[1, kb]
    for chunk in range(32):
        block = back[16 * chunk:16 * chunk + 16]
        co = twist_coarse[chunk, kb]
        si = twist_coarse[chunk, 8 + kb]
        tc = co * fine_c - si * fine_s
        ts = si * fine_c + co * fine_s
        send4[(chunk % 8) * 4 + chunk // 8] = block * tc - sign16 * ts * swap(block)
    rows_exchange(send4, in4, T3P)

    arrived(in4, T3P)
    for ka1 in range(2):
        values = []
        for k in range(8):
            m0, m1 = in4[4 * k + 2 * ka1], in4[4 * k + 2 * ka1 + 1]
            values.append((jnp.where(left16, m0, swap(m1)), jnp.where(left16, swap(m0), m1)))
        for b, (re, im) in enumerate(short_transform(values, 1.0)):
            send5[b, 0, 16 * ka1:16 * ka1 + 16, :] = re
            send5[b, 1, 16 * ka1:16 * ka1 + 16, :] = im

    @pl.loop(0, COLS)
    def _(b):
        mine = self_last & (b == kb)

        @pl.when(mine)
        def _():
            keep(send5.at[b], in5.at[c], T3Q)

        @pl.when(jnp.logical_not(mine))
        def _():
            push(send5.at[b], in5.at[c], T3Q, 4 * b + low2, kb)

    arrived(in5, T3Q)

    pair = jnp.concatenate(
        [in5[:, 0].reshape(256, 128), in5[:, 1].reshape(256, 128)], axis=1
    )
    pair_h, pair_l = split(pair)
    inner = dot3((pair_h, pair_l), (inner_inv[0], inner_inv[1]))
    first = dot3((pair_h[:16], pair_l[:16]), (first_inv[0], first_inv[1]))
    inner = jnp.concatenate([first, inner[16:]], axis=0)
    re, im = inner[:, :128].reshape(16, 16, 128), inner[:, 128:].reshape(16, 16, 128)
    turned = jnp.concatenate(
        [
            (re * tw_c - im * tw_s).reshape(256, 128),
            (im * tw_c + re * tw_s).reshape(256, 128),
        ],
        axis=0,
    )
    final = dot3((outer_inv[0], outer_inv[1]), split(turned))
    for i in range(32):
        map_out[:, pl.ds(128 * i, 128)] = final[16 * i:16 * i + 16]

    for buf, phase in ((in1, T1), (send3, T2B), (send4, T3P), (xp, RP), (xq, RQ), (r1, R1), (r2, R2)):
        left(buf.at[pl.ds(0, ROWS - 1)], phase)
    for buf, phase in ((send2, T2A), (zp, ZP), (zq, ZQ), (z1, Z1), (z2, Z2)):
        left(buf.at[pl.ds(0, COLS - 1)], phase)

    @pl.when(self_last)
    def _():
        left(send5.at[pl.ds(0, COLS - 1)], T3Q)

    @pl.when(jnp.logical_not(self_last))
    def _():
        left(send5, T3Q)

    @pl.when((c == 0) & (low2 == 0))
    def _():
        left(twin_send.at[pl.ds(0, 7)], TWIN)

    @pl.when((c == 0) & (low2 != 0))
    def _():
        left(twin_send, TWIN)

    halo_left(spread0.at[4], ret0, RETURN0, False)
    halo_left(p_own, halo0, COLLECT0, True)
    halo_left(spread1.at[4], ret1, RETURN1, False)
    halo_left(q_own, halo1, COLLECT1, True)


def on_device(
    kernel_tiles, footprints, counts, readings, damping, layer_depth,
    inclinations, declinations, resid_grid,
):
    table = tables()
    foot = footprints.reshape(9)
    nine = jnp.arange(9, dtype=jnp.int32)
    where_code = jnp.sum(jnp.where(foot[:, None] == nine[None, :], nine[:, None], 0), axis=0)
    params = jnp.concatenate(
        [
            damping, layer_depth,
            jnp.sin(inclinations), jnp.cos(inclinations),
            jnp.cos(declinations), jnp.sin(declinations),
        ]
    )
    consts = [jnp.asarray(table[name]) for name in TABLE_NAMES]
    shapes = [x.shape for x in consts]
    shapes[6] = shapes[6][1:]
    shapes[7] = shapes[7][1:]
    kinds = [x.dtype for x in consts]
    smem = pl.BlockSpec(memory_space=pltpu.SMEM)
    vmem = pl.BlockSpec(memory_space=pltpu.VMEM)
    hbm = pl.BlockSpec(memory_space=pl.ANY)

    def v(*shape):
        return pltpu.VMEM(shape, F32)

    block = (32, 16, 128)
    scratch = [v(9, 256, 512)]
    scratch += [pltpu.VMEM(shape, kind) for shape, kind in zip(shapes, kinds)]
    scratch += [
        v(*block), v(8, 32, 256), v(8, 32, 256), v(*block), v(*block),
        v(8, 16, 128), v(*block), v(*block), v(*block), v(8, 2, 32, 128), v(8, 2, 32, 128),
        v(512, 128), v(512, 128), v(8, 512, 128),
    ]
    scratch += [v(9, 8, 128) for _ in range(7)]
    scratch += [
        v(8, 128), v(8, 128), v(8, 8, 128), v(8, 8, 128),
        v(16, 256), v(16, 256), v(32, 16, 256), v(32, 16, 256),
        v(256, 128), v(256, 128), v(8, 128), v(8, 128), v(8, 128), v(8, 128),
        v(8, 8, 128), v(32, 8, 128), v(8, 8, 128), v(32, 8, 128),
    ]
    scratch += [
        pltpu.SemaphoreType.DMA((12,)),
        pltpu.SemaphoreType.DMA((PHASES,)),
        pltpu.SemaphoreType.DMA((PHASES,)),
        pltpu.SemaphoreType.DMA((4, 9)),
        pltpu.SemaphoreType.DMA((4, 9)),
    ]
    coef, rtp_map = pl.pallas_call(
        kernel,
        out_shape=(
            jax.ShapeDtypeStruct((8, 128), F32),
            jax.ShapeDtypeStruct((16, FULL), F32),
        ),
        in_specs=[smem] * 5 + [hbm, vmem, vmem] + [hbm] * len(consts),
        out_specs=(vmem, vmem),
        scratch_shapes=scratch,
        compiler_params=pltpu.CompilerParams(
            collective_id=0, has_side_effects=True, vmem_limit_bytes=60 * 1024 * 1024
        ),
    )(
        foot, where_code, counts.reshape(1), params, jnp.asarray(table["twist_coarse"]),
        kernel_tiles.reshape(9, 256, 512), readings.reshape(1, 256),
        resid_grid.reshape(block), *consts,
    )
    return coef[:4].reshape(1, 1, 512), rtp_map


def solution(mesh):
    in_specs = (
        P("row", "col", None, None, None),
        P("row", "col", None),
        P("row", "col"),
        P("row", "col", None),
        P(),
        P(),
        P(),
        P(),
        P("col", "row"),
    )
    out_specs = (P("row", "col", None), P(("row", "col"), None))
    return jax.shard_map(
        on_device, mesh=mesh, in_specs=in_specs, out_specs=out_specs, check_vma=False
    )
```

```python
import functools
import math

import jax
import jax.numpy as jnp
import ml_dtypes
import numpy as np
from jax import lax
from jax.experimental import pallas as pl
from jax.experimental.pallas import tpu as pltpu
from jax.sharding import PartitionSpec as P

F32 = jnp.float32
BF16 = jnp.bfloat16
MESH = pl.DeviceIdType.MESH
ROWS, COLS = 32, 8
FULL = 4096
REFINE = 16
SLOTS = 256
OFFSETS = tuple((a, b) for a in (-1, 0, 1) for b in (-1, 0, 1))
SCALE = 1.0 / 16777216.0

(T1, T2A, T2B, TWIN, T3P, T3Q, ZP, RP, ZQ, RQ, Z1, R1, Z2, R2) = range(14)
PHASES = 14
RETURN0, COLLECT0, RETURN1, COLLECT1 = range(4)


def halves(x):
    high = x.astype(np.float32).astype(ml_dtypes.bfloat16)
    low = (x - high.astype(np.float64)).astype(np.float32).astype(ml_dtypes.bfloat16)
    return np.stack([high, low])


@functools.lru_cache(maxsize=None)
def tables():
    two_pi = 2.0 * math.pi
    a = np.arange(32)
    ka = np.arange(16)
    n = np.arange(128)
    kn = np.arange(128)
    ang_a = two_pi * np.outer(ka, a) / 32
    outer = np.stack([np.cos(ang_a), -np.sin(ang_a)])
    outer[1, 0] = (-1.0) ** a
    eye = np.eye(16)
    outer_fwd = np.kron(outer.reshape(32, 32), eye)
    inv = np.stack([2 * np.cos(ang_a), -2 * np.sin(ang_a)])
    inv[0, 0] = 1.0
    inv[1, 0] = (-1.0) ** a
    pick = eye.reshape(16, 8, 2)
    outer_inv = np.einsum("qphb,tuv->btpuqhv", inv.reshape(2, 8, 2, 32), pick)
    outer_inv = outer_inv.reshape(512, 512)
    ang_t = two_pi * np.outer(ka, n) / 4096
    twist = np.stack([np.cos(ang_t), np.sin(ang_t)])[:, :, None, :]
    twist_tile = np.broadcast_to(
        np.stack([np.cos(ang_t), np.sin(ang_t)]).reshape(2, 8, 1, 1, 2, 1, 128),
        (2, 8, 1, 2, 2, 2, 128),
    ).reshape(2, 8, 1, 8, 128)
    twist_tile = np.concatenate([twist_tile[:1], twist_tile[1:]])
    th = two_pi * np.outer(n, kn) / 128
    c, s = np.cos(th), np.sin(th)
    inner_fwd = np.block([[c, -s], [s, c]])
    inner_inv = np.concatenate([c.T, s.T], axis=1)
    k0 = np.arange(64)
    th0 = two_pi * np.outer(n, 32 * k0) / 4096
    th1 = two_pi * np.outer(n, 16 + 32 * k0) / 4096
    alt = (-1.0) ** n
    first_fwd = np.zeros((256, 256))
    first_fwd[:128, 0:64] = np.cos(th0)
    first_fwd[:128, 128:192] = -np.sin(th0)
    first_fwd[:128, 128] = alt
    first_fwd[128:, 64:128] = np.cos(th1)
    first_fwd[128:, 192:256] = -np.sin(th1)
    first_inv = np.zeros((256, 256))
    first_inv[0:64, :128] = 2 * np.cos(th0).T
    first_inv[0, :128] = 1.0
    first_inv[128:192, :128] = -2 * np.sin(th0).T
    first_inv[128, :128] = alt
    first_inv[64:128, 128:] = 2 * np.cos(th1).T
    first_inv[192:256, 128:] = -2 * np.sin(th1).T
    first_inv = np.concatenate([first_inv[:128], first_inv[128:]], axis=1)
    w = np.arange(512)
    th_w = two_pi * (np.outer(w, w) % 512) / 512
    east = np.concatenate([np.cos(th_w), np.sin(th_w)])
    back = np.array(
        [
            128 * wh + 16 * wm + 2 * t3 + t1
            for t3 in range(8) for wh in range(4) for t1 in range(2) for wm in range(8)
        ]
    )
    east_inv = np.concatenate([np.cos(th_w)[back], np.sin(th_w)[back]])
    kb = np.arange(8)
    ang_c = two_pi * np.outer(np.arange(32), 16 * kb) / 4096
    twist_coarse = np.concatenate([np.cos(ang_c), np.sin(ang_c)], axis=1)
    ang_f = two_pi * np.outer(kb, np.arange(16)) / 4096
    twist_fine = np.broadcast_to(
        np.stack([np.cos(ang_f), np.sin(ang_f)])[..., None], (2, 8, 16, 128)
    )
    starts = back[::16]
    ang_c = two_pi * np.outer(starts, kb) / 4096
    back_coarse = np.concatenate([np.cos(ang_c), np.sin(ang_c)], axis=1)
    ang_f = two_pi * np.outer(kb, back[:16]) / 4096
    back_fine = np.broadcast_to(
        np.stack([np.cos(ang_f), np.sin(ang_f)])[..., None], (2, 8, 16, 128)
    )
    u = np.arange(4096)
    g = np.arange(256)
    hat = np.maximum(0.0, 1.0 - np.abs((u[:, None] + 0.5) / REFINE - 0.5 - g[None, :]))
    spec = np.fft.fft(hat, axis=0)
    east_hat = np.stack(
        [np.concatenate([spec[k::8].real, spec[k::8].imag]) for k in range(8)]
    )
    order = np.array(
        [8 * i + 4 * m2 + g4 for i in range(32) for g4 in range(4) for m2 in range(2)]
    )
    north_hat = np.zeros((32, 144, 256))
    lane = np.arange(64)
    for col in range(8):
        for ka1 in range(2):
            for knh in range(2):
                slot = 2 * col + ka1
                ku = slot + 32 * (64 * knh + lane) if slot else 16 * knh + 32 * lane
                idx = col * 4 + ka1 * 2 + knh
                north_hat[idx, :64] = spec[ku].real[:, order]
                north_hat[idx, 64:128] = spec[ku].imag[:, order]
    north_hat[0, 128] = spec[2048].real[order]
    f32 = np.float32
    return dict(
        outer_fwd=halves(outer_fwd),
        outer_inv=halves(outer_inv),
        inner_fwd=halves(inner_fwd),
        inner_inv=halves(inner_inv),
        first_fwd=halves(first_fwd),
        first_inv=halves(first_inv),
        east=halves(east),
        east_inv=halves(east_inv),
        twist_tile=np.ascontiguousarray(twist_tile).astype(f32),
        back_fine=np.ascontiguousarray(back_fine).astype(f32),
        back_coarse=back_coarse.astype(f32),
        twist=twist.astype(f32),
        twist_fine=np.ascontiguousarray(twist_fine).astype(f32),
        twist_coarse=twist_coarse.astype(f32),
        east_hat=np.ascontiguousarray(halves(east_hat).swapaxes(0, 1)),
        north_hat=np.ascontiguousarray(halves(north_hat).swapaxes(0, 1)),
    )


TABLE_NAMES = (
    "outer_fwd",
    "inner_fwd",
    "first_fwd",
    "twist",
    "twist_fine",
    "east",
    "north_hat",
    "east_hat",
    "inner_inv",
    "first_inv",
    "outer_inv",
    "east_inv",
    "twist_tile",
    "back_fine",
)


def split(x):
    high = x.astype(BF16)
    return high, (x - high.astype(F32)).astype(BF16)


def dot3(lhs, rhs, transposed=False):
    dims = (((1,), (1 if transposed else 0,)), ((), ()))

    def one(x, y):
        return lax.dot_general(x, y, dims, preferred_element_type=F32)

    return one(lhs[0], rhs[0]) + (one(lhs[0], rhs[1]) + one(lhs[1], rhs[0]))


def short_transform(values, sign):
    count = len(values)
    if count == 1:
        return values
    even = short_transform(values[0::2], sign)
    odd = short_transform(values[1::2], sign)
    out = [None] * count
    for k in range(count // 2):
        re, im = odd[k]
        if k == 0:
            pass
        elif 4 * k == count:
            re, im = -sign * im, sign * re
        else:
            co = math.cos(2 * math.pi * k / count)
            si = sign * math.sin(2 * math.pi * k / count)
            re, im = re * co - im * si, re * si + im * co
        ere, eim = even[k]
        out[k] = (ere + re, eim + im)
        out[k + count // 2] = (ere - re, eim - im)
    return out


def pole_of(fn, fe, angles):
    radius = jnp.sqrt(fn * fn + fe * fe)
    safe = jnp.where(radius > 0.0, radius, 1.0)
    nn = jnp.where(radius > 0.0, fn / safe, 0.0)
    ne = jnp.where(radius > 0.0, fe / safe, 0.0)
    re = im = None
    for m in range(2):
        vertical = angles[m]
        horizontal = angles[2 + m]
        along = horizontal * (angles[4 + m] * nn + angles[6 + m] * ne)
        inverse = 1.0 / (vertical * vertical + along * along)
        one_re, one_im = vertical * inverse, -along * inverse
        if re is None:
            re, im = one_re, one_im
        else:
            re, im = re * one_re - im * one_im, re * one_im + im * one_re
    return re, im, radius


def lanes_of(shape):
    return lax.broadcasted_iota(jnp.int32, shape, len(shape) - 1)


def signs_of(shape):
    return jnp.where(lanes_of(shape) < 64, 1.0, -1.0).astype(F32)


def swap(x):
    return pltpu.roll(x, 64, axis=x.ndim - 1)


def kernel(
    foot, counts, damping, depth, inclinations, declinations, twist_coarse, back_coarse,
    tiles_hbm, readings, grid,
    outer_fwd_h, inner_fwd_h, first_fwd_h, twist_h, twist_fine_h, east_h,
    north_hat_h, east_hat_h, inner_inv_h, first_inv_h, outer_inv_h,
    east_inv_h, twist_tile_h, back_fine_h,
    coef_out, map_out,
    tiles, outer_fwd, inner_fwd, first_fwd, twist, twist_fine, east,
    north_hat, east_hat, inner_inv, first_inv, outer_inv,
    east_inv, twist_tile, back_fine,
    in1, send2, in2, send3, in3, twin_send, twin_in, send4, in4, send5, in5,
    spec_main, spec_twin, filt,
    spread0, spread1, ret0, ret1, halo0, halo1, chosen,
    p_own, q_own, zp, zq, xp_send, xq_send, xp, xq,
    y_p, y_q, sum1, sum2, sum1b, sum2b, z1, r1, z2, r2,
    load_sem, send_sem, recv_sem, halo_send, halo_recv,
):
    r = lax.axis_index("row")
    c = lax.axis_index("col")
    kb = r // 4
    low2 = r % 4
    special = (c == 0) & (low2 == 0)

    loads = [
        (tiles_hbm, tiles),
        (outer_fwd_h, outer_fwd),
        (inner_fwd_h, inner_fwd),
        (first_fwd_h, first_fwd),
        (twist_h, twist),
        (twist_fine_h, twist_fine),
        (east_h, east),
        (north_hat_h.at[c * 4 + low2], north_hat),
        (east_hat_h.at[kb], east_hat),
        (inner_inv_h, inner_inv),
        (first_inv_h, first_inv),
        (outer_inv_h, outer_inv),
        (east_inv_h, east_inv),
        (twist_tile_h, twist_tile),
        (back_fine_h, back_fine),
    ]
    copies = [
        pltpu.make_async_copy(src, dst, load_sem.at[i]) for i, (src, dst) in enumerate(loads)
    ]
    for one in copies:
        one.start()

    barrier = pltpu.get_barrier_semaphore()

    def greet(row, col):
        pl.semaphore_signal(barrier, inc=1, device_id=(row, col), device_id_type=MESH)

    def exists(a, b):
        return (r + a >= 0) & (r + a < ROWS) & (c + b >= 0) & (c + b < COLS)

    @pl.loop(1, ROWS)
    def _(i):
        greet((r + i) % ROWS, c)

    @pl.loop(1, COLS)
    def _(i):
        greet(r, (c + i) % COLS)

    expected = jnp.int32(ROWS - 1 + COLS - 1)
    for a in (-1, 1):
        for b in (-1, 1):
            there = exists(a, b)
            expected = expected + there.astype(jnp.int32)

            @pl.when(there)
            def _():
                greet(r + a, c + b)


    def push(src, dst, phase, row, col):
        pltpu.make_async_remote_copy(
            src_ref=src, dst_ref=dst, send_sem=send_sem.at[phase], recv_sem=recv_sem.at[phase],
            device_id=(row, col), device_id_type=MESH,
        ).start()

    def keep(src, dst, phase):
        pltpu.make_async_copy(src, dst, recv_sem.at[phase]).start()

    def arrived(dst, phase):
        pltpu.make_async_copy(dst, dst, recv_sem.at[phase]).wait()

    def left(ref, phase):
        pltpu.make_async_copy(ref, ref, send_sem.at[phase]).wait()

    def rows_exchange(src, dst, phase):
        keep(src.at[r], dst.at[r], phase)

        @pl.loop(1, ROWS)
        def _(i):
            row = (r + i) % ROWS
            push(src.at[row], dst.at[r], phase, row, c)

    def cols_exchange(src, dst, phase):
        keep(src.at[c], dst.at[c], phase)

        @pl.loop(1, COLS)
        def _(i):
            col = (c + i) % COLS
            push(src.at[col], dst.at[c], phase, r, col)

    def rows_share(src, dst, phase):
        keep(src, dst.at[r], phase)

        @pl.loop(1, ROWS)
        def _(i):
            push(src, dst.at[r], phase, (r + i) % ROWS, c)

    def cols_share(src, dst, phase):
        keep(src, dst.at[c], phase)

        @pl.loop(1, COLS)
        def _(i):
            push(src, dst.at[c], phase, r, (c + i) % COLS)

    def halo_copy(src, dst, turn, code, row, col):
        return pltpu.make_async_remote_copy(
            src_ref=src, dst_ref=dst,
            send_sem=halo_send.at[turn, code], recv_sem=halo_recv.at[turn, code],
            device_id=(row, col), device_id_type=MESH,
        )

    def return_start(spread, dst, turn):
        for code, (a, b) in enumerate(OFFSETS):
            if code != 4:

                @pl.when(exists(a, b))
                def _():
                    halo_copy(spread.at[code], dst.at[code], turn, code, r + a, c + b).start()

    def collect_start(own, dst, turn):
        for code, (a, b) in enumerate(OFFSETS):
            if code != 4:

                @pl.when(exists(-a, -b))
                def _():
                    halo_copy(own, dst.at[code], turn, code, r - a, c - b).start()

    def halo_wait(src, dst, turn, collecting):
        for code, (a, b) in enumerate(OFFSETS):
            if code != 4:
                away = -1 if collecting else 1
                source = exists(-away * a, -away * b)

                @pl.when(source)
                def _():
                    halo_copy(src, dst.at[code], turn, code, r, c).wait_recv()

                @pl.when(jnp.logical_not(source))
                def _():
                    dst[code] = jnp.zeros((8, 128), F32)

    def halo_left(src, dst, turn, collecting):
        for code, (a, b) in enumerate(OFFSETS):
            if code != 4:
                away = -1 if collecting else 1

                @pl.when(exists(away * a, away * b))
                def _():
                    halo_copy(src, dst.at[code], turn, code, r, c).wait_send()

    sub8 = lax.broadcasted_iota(jnp.int32, (8, 128), 0)

    def spread_of(y, out):
        @pl.loop(0, 9)
        def _(code):
            k = jnp.int32(0)
            for j in range(9):
                k = jnp.where(foot[j] == code, j, k)
            total = jnp.zeros((8, 128), F32)
            for m in range(4):
                acc = [jnp.zeros((8, 128), F32) for _ in range(4)]
                for t in range(32):
                    part = tiles[k, pl.ds(8 * t, 8), pl.ds(128 * m, 128)]
                    acc[t % 4] = acc[t % 4] + part * y[pl.ds(8 * t, 8), :]
                row = jnp.sum((acc[0] + acc[1]) + (acc[2] + acc[3]), axis=0, keepdims=True)
                total = total + jnp.where(sub8 == m, jnp.broadcast_to(row, (8, 128)), 0.0)
            out[code] = total

    def readings_of(blocks, y):
        @pl.loop(0, 8)
        def _(chunk):
            base = pl.multiple_of(32 * chunk, 32)
            acc = [jnp.zeros((8, 128), F32) for _ in range(4)]
            for k in range(9):
                code = foot[k]
                for m in range(4):
                    row = jnp.broadcast_to(blocks[code, pl.ds(m, 1), :], (8, 128))
                    for t in range(4):
                        part = tiles[k, pl.ds(base + 8 * t, 8), pl.ds(128 * m, 128)]
                        acc[t] = acc[t] + part * row
            for t in range(4):
                slot = lax.broadcasted_iota(jnp.int32, (8, 128), 0) + (base + 8 * t)
                total = jnp.sum(acc[t], axis=1, keepdims=True)
                y[pl.ds(base + 8 * t, 8), :] = jnp.where(
                    slot < counts[0], jnp.broadcast_to(total, (8, 128)), 0.0
                )

    def gather_blocks(own, halo):
        for code in range(9):
            chosen[code] = own[...] if code == 4 else halo[code]

    def own_sum(spread, ret):
        total = spread[4]
        for code in range(9):
            if code != 4:
                total = total + ret[code]
        return total

    def total_of(x):
        return jnp.sum(jnp.sum(x, axis=1, keepdims=True), axis=0, keepdims=True)

    lane8 = lanes_of((8, 128))

    def pack(parts):
        out = jnp.zeros((8, 128), F32)
        for i, part in enumerate(parts):
            out = out + jnp.where(
                (lane8 == i) & (sub8 == 0), jnp.broadcast_to(part, (8, 128)), 0.0
            )
        return out

    def unpack(x, i):
        return total_of(jnp.where((lane8 == i) & (sub8 == 0), x, 0.0))

    state = {}
    sign512 = signs_of((512, 128))
    left16 = lanes_of((16, 128)) < 64

    def met():
        pl.semaphore_wait(barrier, expected)

    def grid_rows():
        rows_exchange(grid, in1, T1)

    def right_side():
        eye = lax.broadcasted_iota(jnp.int32, (SLOTS, SLOTS), 0) == lanes_of((SLOTS, SLOTS))
        column = jnp.sum(
            jnp.where(eye, jnp.broadcast_to(readings[...], (SLOTS, SLOTS)), 0.0),
            axis=1, keepdims=True,
        )
        slot_index = lax.broadcasted_iota(jnp.int32, (SLOTS, 128), 0)
        y_q[...] = jnp.where(
            slot_index < counts[0], jnp.broadcast_to(column, (SLOTS, 128)), 0.0
        )
        copies[0].wait()
        spread_of(y_q, spread0)

    def right_side_return():
        return_start(spread0, ret0, RETURN0)

    def north_forward():
        for i in range(1, 4):
            copies[i].wait()
        copies[4].wait()
        arrived(in1, T1)
        outer = dot3(
            (outer_fwd[0], outer_fwd[1]), split(in1[...].reshape(512, 128))
        ).reshape(2, 16, 16, 128)
        tw_c, tw_s = twist[0], twist[1]
        turned = jnp.concatenate(
            [
                (outer[0] * tw_c + outer[1] * tw_s).reshape(256, 128),
                (outer[1] * tw_c - outer[0] * tw_s).reshape(256, 128),
            ],
            axis=1,
        )
        turned_h, turned_l = split(turned)
        send2[...] = dot3((turned_h, turned_l), (inner_fwd[0], inner_fwd[1])).reshape(8, 32, 256)
        send2[0, 0:16, :] = dot3((turned_h[:16], turned_l[:16]), (first_fwd[0], first_fwd[1]))
        cols_exchange(send2, in2, T2A)

    def first_direction():
        halo_wait(spread0.at[4], ret0, RETURN0, False)
        p_own[...] = own_sum(spread0, ret0)
        collect_start(p_own, halo0, COLLECT0)
        cols_share(p_own, zp, ZP)

    def first_image():
        halo_wait(p_own, halo0, COLLECT0, True)
        gather_blocks(p_own, halo0)
        readings_of(chosen, y_p)
        p_val = p_own[...]
        sum1[...] = pack([total_of(y_p[...] * y_p[...]) * (1.0 / 128.0), total_of(p_val * p_val)])
        cols_share(sum1, z1, Z1)
        spread_of(y_p, spread1)
        return_start(spread1, ret1, RETURN1)

    lane_half = lanes_of((8, 128)) // 32

    def coarse_rows(z, out):
        for half in range(2):
            for g in range(4):
                total = jnp.zeros((8, 128), F32)
                for j in range(4):
                    block = z[4 * half + j]
                    shift = (32 * (j - g)) % 128
                    if shift:
                        block = pltpu.roll(block, shift, axis=1)
                    total = jnp.where(lane_half == j, block, total)
                lanes = pl.ds(128 * half, 128)
                out[pl.ds(2 * g, 2), lanes] = total[0:2]
                out[pl.ds(8 + 2 * g, 2), lanes] = total[2:4]

    def first_coarse():
        arrived(zp, ZP)
        coarse_rows(zp, xp_send)
        rows_share(xp_send, xp, RP)

    def east_first():
        copies[5].wait()
        arrived(in2, T2A)
        pairs = short_transform(
            [(in2[b, :, 0:128], in2[b, :, 128:256]) for b in range(8)], -1.0
        )
        lane32 = lanes_of((32, 128))
        sub32 = lax.broadcasted_iota(jnp.int32, (32, 128), 0)
        apart = (lane32 == 0) & (sub32 < 16) & (c == 0)
        for k in range(8):
            re, im = pairs[k]
            other_re, other_im = pairs[(8 - k) % 8]
            main_re = jnp.where(apart, 0.5 * (re + other_re), re)
            main_im = jnp.where(apart, 0.5 * (im - other_im), im)
            twin_re = 0.5 * (im[:16] + other_im[:16])
            twin_im = 0.5 * (other_re[:16] - re[:16])
            co = twist_coarse[r, k]
            si = twist_coarse[r, 8 + k]
            fine_c, fine_s = twist_fine[0, k], twist_fine[1, k]
            tc = co * fine_c - si * fine_s
            ts = si * fine_c + co * fine_s
            for ka1 in range(2):
                xr, xi = main_re[16 * ka1:16 * ka1 + 16], main_im[16 * ka1:16 * ka1 + 16]
                yr, yi = xr * tc + xi * ts, xi * tc - xr * ts
                send3[4 * k + 2 * ka1] = jnp.where(left16, yr, swap(yi))
                send3[4 * k + 2 * ka1 + 1] = jnp.where(left16, swap(yr), yi)
            yr, yi = twin_re * tc + twin_im * ts, twin_im * tc - twin_re * ts
            twin_send[k] = jnp.where(left16, yr, swap(yi))
        rows_exchange(send3, in3, T2B)

        @pl.when(c == 0)
        def _():
            @pl.loop(0, 8)
            def _(k):
                @pl.when(4 * k == r)
                def _():
                    keep(twin_send.at[k], twin_in.at[r], TWIN)

                @pl.when(4 * k != r)
                def _():
                    push(twin_send.at[k], twin_in.at[r], TWIN, 4 * k, c)

    def share_sums(z, mine, out, phase_in, phase_out):
        arrived(z, phase_in)
        half_sum = z[0]
        for i in range(1, 8):
            half_sum = half_sum + z[i]
        mine[...] = half_sum
        rows_share(mine, out, phase_out)

    def first_applied():
        halo_wait(spread1.at[4], ret1, RETURN1, False)
        q_own[...] = own_sum(spread1, ret1) + damping[0] * p_own[...]
        collect_start(q_own, halo1, COLLECT1)
        cols_share(q_own, zq, ZQ)

    def first_sums():
        share_sums(z1, sum1b, r1, Z1, R1)

    def second_image():
        halo_wait(q_own, halo1, COLLECT1, True)
        gather_blocks(q_own, halo1)
        readings_of(chosen, y_q)

    def second_coarse():
        arrived(zq, ZQ)
        coarse_rows(zq, xq_send)
        rows_share(xq_send, xq, RQ)

    def first_step():
        arrived(r1, R1)
        weight = damping[0]
        full_sum = jnp.sum(r1[...], axis=0)
        g00, rr0 = unpack(full_sum, 0), unpack(full_sum, 1)
        step0 = rr0 / (g00 + weight * rr0)
        p_val = p_own[...]
        resid = p_val - step0 * q_own[...]
        yr1 = y_p[...] - step0 * y_q[...]
        sum2[...] = pack(
            [
                total_of(yr1 * yr1) * (1.0 / 128.0),
                total_of(yr1 * y_p[...]) * (1.0 / 128.0),
                total_of(resid * resid),
                total_of(resid * p_val),
            ]
        )
        cols_share(sum2, z2, Z2)
        state.update(step0=step0, p_val=p_val, resid=resid, g00=g00, rr0=rr0)

    def second_sums():
        share_sums(z2, sum2b, r2, Z2, R2)

    def filter_tables():
        knh = low2 % 2
        ka = 2 * c + low2 // 2
        given = [inclinations[0], inclinations[1], declinations[0], declinations[1]]
        spot = jnp.zeros((8, 128), F32)
        for i, one in enumerate(given):
            spot = jnp.where(lane8 == i, one, spot)
        sines, cosines = jnp.sin(spot), jnp.cos(spot)

        def taken(x, i):
            return jnp.max(jnp.where(lane8 == i, x, -2.0)[0:1], axis=1, keepdims=True)

        angles = [taken(sines, 0), taken(sines, 1), taken(cosines, 0), taken(cosines, 1)]
        angles += [taken(cosines, 2), taken(cosines, 3), taken(sines, 2), taken(sines, 3)]

        @pl.loop(0, 16)
        def _(chunk):
            base = pl.multiple_of(32 * chunk, 32)
            shape = (32, 128)
            lane = lanes_of(shape)
            kv = kb + 8 * (lax.broadcasted_iota(jnp.int32, shape, 0) + base)
            ku = jnp.where(ka > 0, ka + 32 * (64 * knh + lane), 16 * knh + 32 * lane)
            ku = jnp.where(lane < 64, ku, 2048)
            fe = jnp.where(kv < 2048, kv, kv - 4096).astype(F32) * (1.0 / 4096.0)
            fn = jnp.where(ku < 2048, ku, ku - 4096).astype(F32) * (1.0 / 4096.0)
            re_a, im_a, radius = pole_of(fn, fe, angles)
            re_b, im_b, _ = pole_of(
                jnp.where(ku == 2048, 0.5, fn), jnp.where(kv == 2048, 0.5, fe), angles
            )
            kappa = (2.0 * math.pi) * radius
            made = [
                (0.5 * SCALE) * (re_a + re_b),
                (0.5 * SCALE) * (im_a + im_b),
                jnp.exp(-kappa * depth[0]),
                jnp.exp(-kappa * depth[1]),
            ]
            for i, one in enumerate(made):
                other = swap(one)
                main = jnp.where(lane < 64, one, other)
                twin = jnp.where(lane < 64, other, one)
                if i == 1:
                    sign = signs_of(shape)
                    main, twin = main * sign, twin * sign
                filt[i, pl.ds(base, 32), :] = main
                filt[4 + i, pl.ds(base, 32), :] = twin

    def east_second():
        copies[6].wait()
        arrived(in3, T2B)

        @pl.when(special)
        def _():
            arrived(twin_in, TWIN)

        @pl.when(jnp.logical_not(special))
        def _():
            twin_in[...] = jnp.zeros((32, 16, 128), F32)

        both = jnp.concatenate(
            [in3[...].reshape(512, 128), twin_in[...].reshape(512, 128)], axis=1
        )
        spun = dot3((east[0], east[1]), split(both))
        spec_main[...] = spun[:512, :128] + sign512 * swap(spun[512:, :128])
        spec_twin[...] = spun[:512, 128:] + sign512 * swap(spun[512:, 128:])

    def second_step():
        arrived(xp, RP)
        arrived(xq, RQ)
        arrived(r2, R2)
        step0, p_val, resid = state["step0"], state["p_val"], state["resid"]
        g00, rr0 = state["g00"], state["rr0"]
        full_sum = jnp.sum(r2[...], axis=0)
        g11, g10 = unpack(full_sum, 0), unpack(full_sum, 1)
        rr1, r10 = unpack(full_sum, 2), unpack(full_sum, 3)
        beta = rr1 / rr0
        bent = (g11 + 2.0 * beta * g10 + beta * beta * g00) + damping[0] * (
            rr1 + 2.0 * beta * r10 + beta * beta * rr0
        )
        step1 = rr1 / bent
        coefs = step0 * p_val + step1 * (resid + beta * p_val)
        for m in range(4):
            coef_out[0, :, pl.ds(128 * m, 128)] = coefs[m:m + 1]
        state.update(alpha=step0 + step1 + step1 * beta, gamma=-step1 * step0)

    def shape_spectrum():
        copies[7].wait()
        copies[8].wait()
        copies[12].wait()
        copies[14].wait()
        alpha, gamma = state["alpha"], state["gamma"]
        rows_of = []
        extra = []
        for layer in range(2):
            coarse = alpha * xp[:, 8 * layer:8 * layer + 8, :].reshape(256, 256) + gamma * xq[
                :, 8 * layer:8 * layer + 8, :
            ].reshape(256, 256)
            north = dot3((north_hat[0], north_hat[1]), split(coarse))
            rows_of.append(north[:128])
            extra.append(north[128:144])
        rows_of.extend(extra)
        rows_of.append(jnp.zeros((96, 256), F32))
        model = dot3(
            (east_hat[0], east_hat[1]), split(jnp.concatenate(rows_of, axis=0)), transposed=True
        )
        left512 = lanes_of((512, 128)) < 64
        total = spec_main[...]
        twin = spec_twin[...]
        for layer in range(2):
            lanes = slice(128 * layer, 128 * layer + 128)
            plane = model[:512, lanes] - sign512 * swap(model[512:, lanes])
            total = total + filt[2 + layer] * plane
            top, bottom = model[:512, 256:], model[512:, 256:]
            if layer:
                top = pltpu.roll(top, 112, axis=1)
                bottom = pltpu.roll(bottom, 112, axis=1)
            twin = twin + filt[6 + layer] * jnp.where(left512, top, swap(bottom))
        shaped = filt[0] * total - filt[1] * swap(total)
        shaped_twin = filt[4] * twin - filt[5] * swap(twin)
        joined = special & (lanes_of((512, 128)) % 64 == 0)
        state["shaped"] = shaped - jnp.where(joined, sign512 * swap(shaped_twin), 0.0)

    def east_back():
        spun = dot3((east_inv[0], east_inv[1]), split(state["shaped"]))
        back = spun[:512] - sign512 * swap(spun[512:])
        sign16 = signs_of((16, 128))
        fine_c, fine_s = back_fine[0, kb], back_fine[1, kb]
        for chunk in range(32):
            block = back[16 * chunk:16 * chunk + 16]
            co = back_coarse[chunk, kb]
            si = back_coarse[chunk, 8 + kb]
            tc = co * fine_c - si * fine_s
            ts = si * fine_c + co * fine_s
            send4[chunk] = block * tc - sign16 * ts * swap(block)
        rows_exchange(send4, in4, T3P)

    def east_last():
        arrived(in4, T3P)
        for ka1 in range(2):
            values = []
            for k in range(8):
                m0, m1 = in4[4 * k + 2 * ka1], in4[4 * k + 2 * ka1 + 1]
                values.append((jnp.where(left16, m0, swap(m1)), jnp.where(left16, swap(m0), m1)))
            for b, (re, im) in enumerate(short_transform(values, 1.0)):
                for t1 in range(2):
                    rows = slice(8 * t1, 8 * t1 + 8)
                    send5[b, pl.ds(2 * ka1 + t1, 8, stride=8), :] = re[rows]
                    send5[b, pl.ds(4 + 2 * ka1 + t1, 8, stride=8), :] = im[rows]

        def tile(b, wm):
            return send5.at[b, pl.ds(pl.multiple_of(8 * wm, 8), 8)]

        keep(tile(kb, c), in5.at[c, kb], T3Q)

        @pl.loop(1, 64)
        def _(i):
            b = (kb + i // 8) % COLS
            wm = (c + i) % COLS
            push(tile(b, wm), in5.at[c, kb], T3Q, 4 * b + low2, wm)

    def north_back():
        for i in range(9, 12):
            copies[i].wait()
        copies[13].wait()
        arrived(in5, T3Q)
        halves_in = split(in5[...].reshape(512, 128))
        inner = dot3(halves_in, (inner_inv[0], inner_inv[1]))
        first = dot3((halves_in[0][:64], halves_in[1][:64]), (first_inv[0], first_inv[1]))
        shape = (64, 8, 128)
        row = lax.broadcasted_iota(jnp.int32, shape, 1)
        sign = jnp.where(row < 4, -1.0, 1.0)

        def cross(x):
            return pltpu.roll(x, 4, axis=1)

        both = inner[:, :128].reshape(shape) + sign * cross(inner[:, 128:].reshape(shape))
        rr, ri, ir, ii = [first[:, 128 * i:128 * i + 128].reshape(8, 8, 128) for i in range(4)]
        low = row[:8] < 4
        joint = jnp.where(low, rr + cross(ir), ii + cross(ri))
        both = jnp.concatenate([jnp.where(row[:8] % 4 < 2, joint, both[:8]), both[8:]], axis=0)
        shape = (8, 8, 8, 128)
        turned = both.reshape(shape) * twist_tile[0] + (sign * cross(both)).reshape(
            shape
        ) * twist_tile[1]
        final = dot3((outer_inv[0], outer_inv[1]), split(turned.reshape(512, 128)))
        for i in range(32):
            map_out[:, pl.ds(128 * i, 128)] = final[16 * i:16 * i + 16]

    filter_tables()
    right_side()
    met()
    grid_rows()
    right_side_return()
    north_forward()
    first_direction()
    first_image()
    first_coarse()
    east_first()
    first_applied()
    first_sums()
    second_image()
    second_coarse()
    first_step()
    east_second()
    second_sums()
    second_step()
    shape_spectrum()
    east_back()
    east_last()
    north_back()

    for buf, phase in ((in1, T1), (send3, T2B), (send4, T3P), (xp, RP), (xq, RQ), (r1, R1), (r2, R2)):
        left(buf.at[pl.ds(0, ROWS - 1)], phase)
    for buf, phase in ((send2, T2A), (zp, ZP), (zq, ZQ), (z1, Z1), (z2, Z2)):
        left(buf.at[pl.ds(0, COLS - 1)], phase)

    left(send5.at[pl.ds(0, 7)], T3Q)
    left(send5.at[0, pl.ds(0, 56)], T3Q)

    @pl.when((c == 0) & (low2 == 0))
    def _():
        left(twin_send.at[pl.ds(0, 7)], TWIN)

    @pl.when((c == 0) & (low2 != 0))
    def _():
        left(twin_send, TWIN)

    halo_left(spread0.at[4], ret0, RETURN0, False)
    halo_left(p_own, halo0, COLLECT0, True)
    halo_left(spread1.at[4], ret1, RETURN1, False)
    halo_left(q_own, halo1, COLLECT1, True)


def on_device(
    kernel_tiles, footprints, counts, readings, damping, layer_depth,
    inclinations, declinations, resid_grid,
):
    table = tables()
    consts = [jnp.asarray(table[name]) for name in TABLE_NAMES]
    shapes = [x.shape for x in consts]
    shapes[6] = shapes[6][1:]
    shapes[7] = shapes[7][1:]
    kinds = [x.dtype for x in consts]
    smem = pl.BlockSpec(memory_space=pltpu.SMEM)
    vmem = pl.BlockSpec(memory_space=pltpu.VMEM)
    hbm = pl.BlockSpec(memory_space=pl.ANY)

    def v(*shape):
        return pltpu.VMEM(shape, F32)

    block = (32, 16, 128)
    scratch = [v(9, 256, 512)]
    scratch += [pltpu.VMEM(shape, kind) for shape, kind in zip(shapes, kinds)]
    scratch += [
        v(*block), v(8, 32, 256), v(8, 32, 256), v(*block), v(*block),
        v(8, 16, 128), v(*block), v(*block), v(*block), v(8, 64, 128), v(8, 8, 8, 128),
        v(512, 128), v(512, 128), v(8, 512, 128),
    ]
    scratch += [v(9, 8, 128) for _ in range(7)]
    scratch += [
        v(8, 128), v(8, 128), v(8, 8, 128), v(8, 8, 128),
        v(16, 256), v(16, 256), v(32, 16, 256), v(32, 16, 256),
        v(256, 128), v(256, 128), v(8, 128), v(8, 128), v(8, 128), v(8, 128),
        v(8, 8, 128), v(32, 8, 128), v(8, 8, 128), v(32, 8, 128),
    ]
    scratch += [
        pltpu.SemaphoreType.DMA((15,)),
        pltpu.SemaphoreType.DMA((PHASES,)),
        pltpu.SemaphoreType.DMA((PHASES,)),
        pltpu.SemaphoreType.DMA((4, 9)),
        pltpu.SemaphoreType.DMA((4, 9)),
    ]
    coef, rtp_map = pl.pallas_call(
        kernel,
        out_shape=(
            jax.ShapeDtypeStruct((1, 1, 512), F32),
            jax.ShapeDtypeStruct((16, FULL), F32),
        ),
        in_specs=[smem] * 8 + [hbm, vmem, vmem] + [hbm] * len(consts),
        out_specs=(vmem, vmem),
        scratch_shapes=scratch,
        compiler_params=pltpu.CompilerParams(
            collective_id=0, has_side_effects=True, vmem_limit_bytes=60 * 1024 * 1024
        ),
    )(
        footprints.reshape(9), counts.reshape(1), damping, layer_depth,
        inclinations, declinations,
        jnp.asarray(table["twist_coarse"]), jnp.asarray(table["back_coarse"]),
        kernel_tiles.reshape(9, 256, 512), readings.reshape(1, 256),
        resid_grid.reshape(block), *consts,
    )
    return coef, rtp_map


def solution(mesh):
    in_specs = (
        P("row", "col", None, None, None),
        P("row", "col", None),
        P("row", "col"),
        P("row", "col", None),
        P(),
        P(),
        P(),
        P(),
        P("col", "row"),
    )
    out_specs = (P("row", "col", None), P(("row", "col"), None))
    return jax.shard_map(
        on_device, mesh=mesh, in_specs=in_specs, out_specs=out_specs, check_vma=False
    )
```

```python
import functools
import math

import jax
import jax.numpy as jnp
import ml_dtypes
import numpy as np
from jax import lax
from jax.experimental import pallas as pl
from jax.experimental.pallas import tpu as pltpu
from jax.sharding import PartitionSpec as P

F32 = jnp.float32
BF16 = jnp.bfloat16
MESH = pl.DeviceIdType.MESH
ROWS, COLS = 32, 8
FULL = 4096
REFINE = 16
SLOTS = 256
OFFSETS = tuple((a, b) for a in (-1, 0, 1) for b in (-1, 0, 1))
SCALE = 1.0 / 16777216.0

(T1, T2A, T2B, TWIN, T3P, T3Q, ZP, RP, ZQ, RQ, Z1, R1, Z2, R2, RP2, RQ2) = range(16)
PHASES = 16
RETURN0, COLLECT0, RETURN1, COLLECT1 = range(4)


def halves(x):
    high = x.astype(np.float32).astype(ml_dtypes.bfloat16)
    low = (x - high.astype(np.float64)).astype(np.float32).astype(ml_dtypes.bfloat16)
    return np.stack([high, low])


@functools.lru_cache(maxsize=None)
def tables():
    two_pi = 2.0 * math.pi
    a = np.arange(32)
    ka = np.arange(16)
    n = np.arange(128)
    kn = np.arange(128)
    ang_a = two_pi * np.outer(ka, a) / 32
    outer = np.stack([np.cos(ang_a), -np.sin(ang_a)])
    outer[1, 0] = (-1.0) ** a
    eye = np.eye(16)
    outer_fwd = np.kron(outer.reshape(32, 32), eye)
    inv = np.stack([2 * np.cos(ang_a), -2 * np.sin(ang_a)])
    inv[0, 0] = 1.0
    inv[1, 0] = (-1.0) ** a
    outer_inv = np.kron(inv.reshape(32, 32).T, eye)
    ang_t = two_pi * np.outer(ka, n) / 4096
    twist = np.stack([np.cos(ang_t), np.sin(ang_t)])[:, :, None, :]
    th = two_pi * np.outer(n, kn) / 128
    c, s = np.cos(th), np.sin(th)
    inner_fwd = np.block([[c, -s], [s, c]])
    inner_inv = np.block([[c.T, s.T], [-s.T, c.T]])
    k0 = np.arange(64)
    th0 = two_pi * np.outer(n, 32 * k0) / 4096
    th1 = two_pi * np.outer(n, 16 + 32 * k0) / 4096
    alt = (-1.0) ** n
    first_fwd = np.zeros((256, 256))
    first_fwd[:128, 0:64] = np.cos(th0)
    first_fwd[:128, 128:192] = -np.sin(th0)
    first_fwd[:128, 128] = alt
    first_fwd[128:, 64:128] = np.cos(th1)
    first_fwd[128:, 192:256] = -np.sin(th1)
    first_inv = np.zeros((256, 256))
    first_inv[0:64, :128] = 2 * np.cos(th0).T
    first_inv[0, :128] = 1.0
    first_inv[128:192, :128] = -2 * np.sin(th0).T
    first_inv[128, :128] = alt
    first_inv[64:128, 128:] = 2 * np.cos(th1).T
    first_inv[192:256, 128:] = -2 * np.sin(th1).T
    by_half = np.concatenate(
        [np.arange(64), 128 + np.arange(64), 64 + np.arange(64), 192 + np.arange(64)]
    )
    inner_inv, first_inv = inner_inv[by_half], first_inv[by_half]
    w = np.arange(512)
    th_w = two_pi * (np.outer(w, w) % 512) / 512
    east = np.concatenate([np.cos(th_w), np.sin(th_w)])
    back = np.arange(512).reshape(4, 8, 16).transpose(1, 0, 2).reshape(512)
    east_inv = np.concatenate([np.cos(th_w)[back], np.sin(th_w)[back]])
    kb = np.arange(8)
    ang_c = two_pi * np.outer(np.arange(32), 16 * kb) / 4096
    twist_coarse = np.concatenate([np.cos(ang_c), np.sin(ang_c)], axis=1)
    ang_f = two_pi * np.outer(kb, np.arange(16)) / 4096
    twist_fine = np.broadcast_to(
        np.stack([np.cos(ang_f), np.sin(ang_f)])[..., None], (2, 8, 16, 128)
    )
    u = np.arange(4096)
    g = np.arange(256)
    hat = np.maximum(0.0, 1.0 - np.abs((u[:, None] + 0.5) / REFINE - 0.5 - g[None, :]))
    spec = np.fft.fft(hat, axis=0)
    east_hat = np.stack(
        [np.concatenate([spec[k::8].real, spec[k::8].imag]) for k in range(8)]
    )
    order = np.array(
        [
            8 * (2 * chip + core) + 4 * m2 + g4
            for core in range(2) for chip in range(16) for g4 in range(4) for m2 in range(2)
        ]
    )
    north_hat = np.zeros((32, 144, 256))
    lane = np.arange(64)
    for col in range(8):
        for ka1 in range(2):
            for knh in range(2):
                slot = 2 * col + ka1
                ku = slot + 32 * (64 * knh + lane) if slot else 16 * knh + 32 * lane
                idx = col * 4 + ka1 * 2 + knh
                north_hat[idx, :64] = spec[ku].real[:, order]
                north_hat[idx, 64:128] = spec[ku].imag[:, order]
    north_hat[0, 128] = spec[2048].real[order]
    f32 = np.float32
    return dict(
        outer_fwd=halves(outer_fwd),
        outer_inv=halves(outer_inv),
        inner_fwd=halves(inner_fwd),
        inner_inv=halves(inner_inv),
        first_fwd=halves(first_fwd),
        first_inv=halves(first_inv),
        east=halves(east),
        east_inv=halves(east_inv),
        twist=twist.astype(f32),
        twist_fine=np.ascontiguousarray(twist_fine).astype(f32),
        twist_coarse=twist_coarse.astype(f32),
        east_hat=np.ascontiguousarray(halves(east_hat).swapaxes(0, 1)),
        north_hat=np.ascontiguousarray(halves(north_hat).swapaxes(0, 1)),
    )


TABLE_NAMES = (
    "outer_fwd",
    "inner_fwd",
    "first_fwd",
    "twist",
    "twist_fine",
    "east",
    "north_hat",
    "east_hat",
    "inner_inv",
    "first_inv",
    "outer_inv",
    "east_inv",
)


def split(x):
    high = x.astype(BF16)
    return high, (x - high.astype(F32)).astype(BF16)


def dot3(lhs, rhs, transposed=False):
    dims = (((1,), (1 if transposed else 0,)), ((), ()))

    def one(x, y):
        return lax.dot_general(x, y, dims, preferred_element_type=F32)

    return one(lhs[0], rhs[0]) + (one(lhs[0], rhs[1]) + one(lhs[1], rhs[0]))


def short_transform(values, sign):
    count = len(values)
    if count == 1:
        return values
    even = short_transform(values[0::2], sign)
    odd = short_transform(values[1::2], sign)
    out = [None] * count
    for k in range(count // 2):
        re, im = odd[k]
        if k == 0:
            pass
        elif 4 * k == count:
            re, im = -sign * im, sign * re
        else:
            co = math.cos(2 * math.pi * k / count)
            si = sign * math.sin(2 * math.pi * k / count)
            re, im = re * co - im * si, re * si + im * co
        ere, eim = even[k]
        out[k] = (ere + re, eim + im)
        out[k + count // 2] = (ere - re, eim - im)
    return out


def pole_of(fn, fe, angles):
    radius = jnp.sqrt(fn * fn + fe * fe)
    safe = jnp.where(radius > 0.0, radius, 1.0)
    nn = jnp.where(radius > 0.0, fn / safe, 0.0)
    ne = jnp.where(radius > 0.0, fe / safe, 0.0)
    re = im = None
    for m in range(2):
        vertical = angles[m]
        horizontal = angles[2 + m]
        along = horizontal * (angles[4 + m] * nn + angles[6 + m] * ne)
        inverse = 1.0 / (vertical * vertical + along * along)
        one_re, one_im = vertical * inverse, -along * inverse
        if re is None:
            re, im = one_re, one_im
        else:
            re, im = re * one_re - im * one_im, re * one_im + im * one_re
    return re, im, radius


def lanes_of(shape):
    return lax.broadcasted_iota(jnp.int32, shape, len(shape) - 1)


def signs_of(shape):
    return jnp.where(lanes_of(shape) < 64, 1.0, -1.0).astype(F32)


def swap(x):
    return pltpu.roll(x, 64, axis=x.ndim - 1)


def kernel(
    foot, counts, damping, depth, inclinations, declinations, twist_coarse,
    tiles_hbm, readings, grid,
    outer_fwd_h, inner_fwd_h, first_fwd_h, twist_h, twist_fine_h, east_h,
    north_hat_h, east_hat_h, inner_inv_h, first_inv_h, outer_inv_h,
    east_inv_h,
    coef_out, map_out,
    tiles, outer_fwd, inner_fwd, first_fwd, twist, twist_fine, east,
    north_hat, east_hat, inner_inv, first_inv, outer_inv,
    east_inv,
    in1, send2, in2, send3, in3, twin_send, twin_in, send4, in4, send5, in5,
    spec_main, spec_twin, filt,
    spread0, spread1, ret0, ret1, halo0, halo1, chosen,
    p_own, q_own, zp, zq, xp_send, xq_send, xp, xq,
    y_p, y_q, sum1, sum2, sum1b, sum2b, z1, r1, z2, r2,
    load_sem, send_sem, recv_sem, halo_send, halo_recv,
):
    r = lax.axis_index("row")
    c = lax.axis_index("col")
    group = r // 4
    low2 = r % 4
    special = r == 0

    loads = [
        (tiles_hbm, tiles),
        (outer_fwd_h, outer_fwd),
        (inner_fwd_h, inner_fwd),
        (first_fwd_h, first_fwd),
        (twist_h, twist),
        (twist_fine_h, twist_fine),
        (east_h, east),
        (north_hat_h.at[r], north_hat),
        (east_hat_h.at[c], east_hat),
        (inner_inv_h, inner_inv),
        (first_inv_h, first_inv),
        (outer_inv_h, outer_inv),
        (east_inv_h, east_inv),
    ]
    copies = [
        pltpu.make_async_copy(src, dst, load_sem.at[i]) for i, (src, dst) in enumerate(loads)
    ]
    copies[0].start()

    barrier = pltpu.get_barrier_semaphore()

    def greet(row, col):
        pl.semaphore_signal(barrier, inc=1, device_id=(row, col), device_id_type=MESH)

    def exists(a, b):
        return (r + a >= 0) & (r + a < ROWS) & (c + b >= 0) & (c + b < COLS)

    @pl.loop(1, ROWS)
    def _(i):
        greet((r + i) % ROWS, c)

    @pl.loop(1, COLS)
    def _(i):
        greet(r, (c + i) % COLS)

    expected = jnp.int32(ROWS - 1 + COLS - 1)
    for a in (-1, 1):
        for b in (-1, 1):
            there = exists(a, b)
            expected = expected + there.astype(jnp.int32)

            @pl.when(there)
            def _():
                greet(r + a, c + b)


    def push(src, dst, phase, row, col):
        pltpu.make_async_remote_copy(
            src_ref=src, dst_ref=dst, send_sem=send_sem.at[phase], recv_sem=recv_sem.at[phase],
            device_id=(row, col), device_id_type=MESH,
        ).start()

    def keep(src, dst, phase):
        pltpu.make_async_copy(src, dst, recv_sem.at[phase]).start()

    def arrived(dst, phase):
        pltpu.make_async_copy(dst, dst, recv_sem.at[phase]).wait()

    def left(ref, phase):
        pltpu.make_async_copy(ref, ref, send_sem.at[phase]).wait()

    def far_col(j):
        half = (j + 1) // 2
        return (c + jnp.where(j % 2 == 1, 4 - half, 4 + half)) % COLS

    def far_row(j):
        def step(i):
            return jnp.where(i == 0, 2, jnp.where(i == 3, 0, 2 * i - 1))

        x = (r // 8 + step(j // 8)) % 4
        y = (r // 2 + step(j // 2 % 4)) % 4
        return 8 * x + 2 * y + (r + 1 + j) % 2

    def rows_exchange(src, dst, phase):
        keep(src.at[r], dst.at[r], phase)

        @pl.loop(0, ROWS - 1)
        def _(i):
            row = far_row(i)
            push(src.at[row], dst.at[r], phase, row, c)

    def cols_exchange(src, dst, phase):
        keep(src.at[c], dst.at[c], phase)

        @pl.loop(0, COLS - 1)
        def _(i):
            col = far_col(i)
            push(src.at[col], dst.at[c], phase, r, col)

    def rows_share(src, dst, phase):
        keep(src, dst.at[r], phase)

        @pl.loop(0, ROWS - 1)
        def _(i):
            push(src, dst.at[r], phase, far_row(i), c)

    core = r % 2
    chip = r // 2

    def chips_share(src, dst, phase):
        keep(src, dst.at[core, chip], phase)

        @pl.loop(0, ROWS // 2 - 1)
        def _(i):
            push(src, dst.at[core, chip], phase, far_row(2 * i + 1), c)

    def chip_share(dst, phase_in, phase_out):
        arrived(dst.at[core], phase_in)
        push(dst.at[core], dst.at[core], phase_out, r + 1 - 2 * core, c)

    def cols_share(src, dst, phase):
        keep(src, dst.at[c], phase)

        @pl.loop(0, COLS - 1)
        def _(i):
            push(src, dst.at[c], phase, r, far_col(i))

    def halo_copy(src, dst, turn, code, row, col):
        return pltpu.make_async_remote_copy(
            src_ref=src, dst_ref=dst,
            send_sem=halo_send.at[turn, code], recv_sem=halo_recv.at[turn, code],
            device_id=(row, col), device_id_type=MESH,
        )

    def return_start(spread, dst, turn):
        for code, (a, b) in enumerate(OFFSETS):
            if code != 4:

                @pl.when(exists(a, b))
                def _():
                    halo_copy(spread.at[code], dst.at[code], turn, code, r + a, c + b).start()

    def collect_start(own, dst, turn):
        for code, (a, b) in enumerate(OFFSETS):
            if code != 4:

                @pl.when(exists(-a, -b))
                def _():
                    halo_copy(own, dst.at[code], turn, code, r - a, c - b).start()

    def halo_wait(src, dst, turn, collecting):
        for code, (a, b) in enumerate(OFFSETS):
            if code != 4:
                away = -1 if collecting else 1
                source = exists(-away * a, -away * b)

                @pl.when(source)
                def _():
                    halo_copy(src, dst.at[code], turn, code, r, c).wait_recv()

                @pl.when(jnp.logical_not(source))
                def _():
                    dst[code] = jnp.zeros((8, 128), F32)

    def halo_left(src, dst, turn, collecting):
        for code, (a, b) in enumerate(OFFSETS):
            if code != 4:
                away = -1 if collecting else 1

                @pl.when(exists(away * a, away * b))
                def _():
                    halo_copy(src, dst.at[code], turn, code, r, c).wait_send()

    sub8 = lax.broadcasted_iota(jnp.int32, (8, 128), 0)

    def spread_of(y, out):
        @pl.loop(0, 9)
        def _(code):
            k = jnp.int32(0)
            for j in range(9):
                k = jnp.where(foot[j] == code, j, k)
            total = jnp.zeros((8, 128), F32)
            for m in range(4):
                acc = [jnp.zeros((8, 128), F32) for _ in range(4)]
                for t in range(32):
                    part = tiles[k, pl.ds(8 * t, 8), pl.ds(128 * m, 128)]
                    acc[t % 4] = acc[t % 4] + part * y[pl.ds(8 * t, 8), :]
                row = jnp.sum((acc[0] + acc[1]) + (acc[2] + acc[3]), axis=0, keepdims=True)
                total = total + jnp.where(sub8 == m, jnp.broadcast_to(row, (8, 128)), 0.0)
            out[code] = total

    def readings_of(blocks, y):
        @pl.loop(0, 8)
        def _(chunk):
            base = pl.multiple_of(32 * chunk, 32)
            acc = [jnp.zeros((8, 128), F32) for _ in range(4)]
            for k in range(9):
                code = foot[k]
                for m in range(4):
                    row = jnp.broadcast_to(blocks[code, pl.ds(m, 1), :], (8, 128))
                    for t in range(4):
                        part = tiles[k, pl.ds(base + 8 * t, 8), pl.ds(128 * m, 128)]
                        acc[t] = acc[t] + part * row
            for t in range(4):
                slot = lax.broadcasted_iota(jnp.int32, (8, 128), 0) + (base + 8 * t)
                total = jnp.sum(acc[t], axis=1, keepdims=True)
                y[pl.ds(base + 8 * t, 8), :] = jnp.where(
                    slot < counts[0], jnp.broadcast_to(total, (8, 128)), 0.0
                )

    def gather_blocks(own, halo):
        for code in range(9):
            chosen[code] = own[...] if code == 4 else halo[code]

    def own_sum(spread, ret):
        total = spread[4]
        for code in range(9):
            if code != 4:
                total = total + ret[code]
        return total

    def total_of(x):
        return jnp.sum(jnp.sum(x, axis=1, keepdims=True), axis=0, keepdims=True)

    lane8 = lanes_of((8, 128))

    def pack(parts):
        out = jnp.zeros((8, 128), F32)
        for i, part in enumerate(parts):
            out = out + jnp.where(
                (lane8 == i) & (sub8 == 0), jnp.broadcast_to(part, (8, 128)), 0.0
            )
        return out

    def unpack(x, i):
        return total_of(jnp.where((lane8 == i) & (sub8 == 0), x, 0.0))

    state = {}
    sign512 = signs_of((512, 128))
    left16 = lanes_of((16, 128)) < 64

    def met():
        pl.semaphore_wait(barrier, expected)

    def grid_rows():
        rows_exchange(grid, in1, T1)

    def right_side():
        eye = lax.broadcasted_iota(jnp.int32, (SLOTS, SLOTS), 0) == lanes_of((SLOTS, SLOTS))
        column = jnp.sum(
            jnp.where(eye, jnp.broadcast_to(readings[...], (SLOTS, SLOTS)), 0.0),
            axis=1, keepdims=True,
        )
        slot_index = lax.broadcasted_iota(jnp.int32, (SLOTS, 128), 0)
        y_q[...] = jnp.where(
            slot_index < counts[0], jnp.broadcast_to(column, (SLOTS, 128)), 0.0
        )
        copies[0].wait()
        for one in copies[1:]:
            one.start()
        spread_of(y_q, spread0)

    def right_side_return():
        return_start(spread0, ret0, RETURN0)

    def north_forward():
        for i in range(1, 4):
            copies[i].wait()
        copies[4].wait()
        arrived(in1, T1)
        outer = dot3(
            (outer_fwd[0], outer_fwd[1]), split(in1[...].reshape(512, 128))
        ).reshape(2, 16, 16, 128)
        tw_c, tw_s = twist[0], twist[1]
        turned = jnp.concatenate(
            [
                (outer[0] * tw_c + outer[1] * tw_s).reshape(256, 128),
                (outer[1] * tw_c - outer[0] * tw_s).reshape(256, 128),
            ],
            axis=1,
        )
        turned_h, turned_l = split(turned)
        send2[...] = dot3((turned_h, turned_l), (inner_fwd[0], inner_fwd[1])).reshape(8, 32, 256)
        send2[0, 0:16, :] = dot3((turned_h[:16], turned_l[:16]), (first_fwd[0], first_fwd[1]))
        cols_exchange(send2, in2, T2A)

    def first_direction():
        halo_wait(spread0.at[4], ret0, RETURN0, False)
        p_own[...] = own_sum(spread0, ret0)
        collect_start(p_own, halo0, COLLECT0)
        cols_share(p_own, zp, ZP)

    def first_image():
        halo_wait(p_own, halo0, COLLECT0, True)
        gather_blocks(p_own, halo0)
        readings_of(chosen, y_p)
        p_val = p_own[...]
        sum1[...] = pack([total_of(y_p[...] * y_p[...]) * (1.0 / 128.0), total_of(p_val * p_val)])
        cols_share(sum1, z1, Z1)
        spread_of(y_p, spread1)
        return_start(spread1, ret1, RETURN1)

    lane_half = lanes_of((8, 128)) // 32

    def coarse_rows(z, out):
        for half in range(2):
            for g in range(4):
                total = jnp.zeros((8, 128), F32)
                for j in range(4):
                    block = z[4 * half + j]
                    shift = (32 * (j - g)) % 128
                    if shift:
                        block = pltpu.roll(block, shift, axis=1)
                    total = jnp.where(lane_half == j, block, total)
                lanes = pl.ds(128 * half, 128)
                out[pl.ds(2 * g, 2), lanes] = total[0:2]
                out[pl.ds(8 + 2 * g, 2), lanes] = total[2:4]

    def first_coarse():
        arrived(zp, ZP)
        coarse_rows(zp, xp_send)
        chips_share(xp_send, xp, RP)

    def east_first():
        copies[5].wait()
        arrived(in2, T2A)
        pairs = short_transform(
            [(in2[b, :, 0:128], in2[b, :, 128:256]) for b in range(8)], -1.0
        )
        lane32 = lanes_of((32, 128))
        sub32 = lax.broadcasted_iota(jnp.int32, (32, 128), 0)
        apart = (lane32 == 0) & (sub32 < 16) & (c == 0)
        for k in range(8):
            re, im = pairs[k]
            other_re, other_im = pairs[(8 - k) % 8]
            main_re = jnp.where(apart, 0.5 * (re + other_re), re)
            main_im = jnp.where(apart, 0.5 * (im - other_im), im)
            twin_re = 0.5 * (im[:16] + other_im[:16])
            twin_im = 0.5 * (other_re[:16] - re[:16])
            co = twist_coarse[r, k]
            si = twist_coarse[r, 8 + k]
            fine_c, fine_s = twist_fine[0, k], twist_fine[1, k]
            tc = co * fine_c - si * fine_s
            ts = si * fine_c + co * fine_s
            for ka1 in range(2):
                xr, xi = main_re[16 * ka1:16 * ka1 + 16], main_im[16 * ka1:16 * ka1 + 16]
                yr, yi = xr * tc + xi * ts, xi * tc - xr * ts
                send3[4 * k + 2 * ka1] = jnp.where(left16, yr, swap(yi))
                send3[4 * k + 2 * ka1 + 1] = jnp.where(left16, swap(yr), yi)
            yr, yi = twin_re * tc + twin_im * ts, twin_im * tc - twin_re * ts
            twin_send[k] = jnp.where(left16, yr, swap(yi))
        mine = group == c

        @pl.loop(0, ROWS)
        def _(i):
            k = far_col(i // 4)
            low = (low2 + i) % 4
            block = send3.at[4 * k + low]

            @pl.when(mine & (k == c) & (low == low2))
            def _():
                keep(block, in3.at[r], T2B)

            @pl.when(jnp.logical_not(mine & (k == c) & (low == low2)))
            def _():
                push(block, in3.at[r], T2B, 4 * c + low, k)

        @pl.when(c == 0)
        def _():
            @pl.loop(0, COLS)
            def _(k):
                @pl.when((k == 0) & (r == 0))
                def _():
                    keep(twin_send.at[k], twin_in.at[r], TWIN)

                @pl.when(jnp.logical_not((k == 0) & (r == 0)))
                def _():
                    push(twin_send.at[k], twin_in.at[r], TWIN, 0, k)

    def share_sums(z, mine, out, phase_in, phase_out):
        arrived(z, phase_in)
        half_sum = z[0]
        for i in range(1, 8):
            half_sum = half_sum + z[i]
        mine[...] = half_sum
        rows_share(mine, out, phase_out)

    def first_applied():
        halo_wait(spread1.at[4], ret1, RETURN1, False)
        q_own[...] = own_sum(spread1, ret1) + damping[0] * p_own[...]
        collect_start(q_own, halo1, COLLECT1)
        cols_share(q_own, zq, ZQ)

    def first_spread():
        chip_share(xp, RP, RP2)

    def second_spread():
        chip_share(xq, RQ, RQ2)

    def first_sums():
        share_sums(z1, sum1b, r1, Z1, R1)

    def second_image():
        halo_wait(q_own, halo1, COLLECT1, True)
        gather_blocks(q_own, halo1)
        readings_of(chosen, y_q)

    def second_coarse():
        arrived(zq, ZQ)
        coarse_rows(zq, xq_send)
        chips_share(xq_send, xq, RQ)

    def first_step():
        arrived(r1, R1)
        weight = damping[0]
        full_sum = jnp.sum(r1[...], axis=0)
        g00, rr0 = unpack(full_sum, 0), unpack(full_sum, 1)
        step0 = rr0 / (g00 + weight * rr0)
        p_val = p_own[...]
        resid = p_val - step0 * q_own[...]
        yr1 = y_p[...] - step0 * y_q[...]
        sum2[...] = pack(
            [
                total_of(yr1 * yr1) * (1.0 / 128.0),
                total_of(yr1 * y_p[...]) * (1.0 / 128.0),
                total_of(resid * resid),
                total_of(resid * p_val),
            ]
        )
        cols_share(sum2, z2, Z2)
        state.update(step0=step0, p_val=p_val, resid=resid, g00=g00, rr0=rr0)

    def second_sums():
        share_sums(z2, sum2b, r2, Z2, R2)

    def filter_tables():
        knh = low2 % 2
        ka = 2 * group + low2 // 2
        given = [inclinations[0], inclinations[1], declinations[0], declinations[1]]
        spot = jnp.zeros((8, 128), F32)
        for i, one in enumerate(given):
            spot = jnp.where(lane8 == i, one, spot)
        sines, cosines = jnp.sin(spot), jnp.cos(spot)

        def taken(x, i):
            return jnp.max(jnp.where(lane8 == i, x, -2.0)[0:1], axis=1, keepdims=True)

        angles = [taken(sines, 0), taken(sines, 1), taken(cosines, 0), taken(cosines, 1)]
        angles += [taken(cosines, 2), taken(cosines, 3), taken(sines, 2), taken(sines, 3)]

        @pl.loop(0, 16)
        def _(chunk):
            base = pl.multiple_of(32 * chunk, 32)
            shape = (32, 128)
            lane = lanes_of(shape)
            kv = c + 8 * (lax.broadcasted_iota(jnp.int32, shape, 0) + base)
            ku = jnp.where(ka > 0, ka + 32 * (64 * knh + lane), 16 * knh + 32 * lane)
            ku = jnp.where(lane < 64, ku, 2048)
            fe = jnp.where(kv < 2048, kv, kv - 4096).astype(F32) * (1.0 / 4096.0)
            fn = jnp.where(ku < 2048, ku, ku - 4096).astype(F32) * (1.0 / 4096.0)
            re_a, im_a, radius = pole_of(fn, fe, angles)
            re_b, im_b, _ = pole_of(
                jnp.where(ku == 2048, 0.5, fn), jnp.where(kv == 2048, 0.5, fe), angles
            )
            kappa = (2.0 * math.pi) * radius
            made = [
                (0.5 * SCALE) * (re_a + re_b),
                (0.5 * SCALE) * (im_a + im_b),
                jnp.exp(-kappa * depth[0]),
                jnp.exp(-kappa * depth[1]),
            ]
            for i, one in enumerate(made):
                other = swap(one)
                main = jnp.where(lane < 64, one, other)
                twin = jnp.where(lane < 64, other, one)
                if i == 1:
                    sign = signs_of(shape)
                    main, twin = main * sign, twin * sign
                filt[i, pl.ds(base, 32), :] = main
                filt[4 + i, pl.ds(base, 32), :] = twin

    def east_second():
        copies[6].wait()
        arrived(in3, T2B)

        @pl.when(special)
        def _():
            arrived(twin_in, TWIN)

        @pl.when(jnp.logical_not(special))
        def _():
            twin_in[...] = jnp.zeros((32, 16, 128), F32)

        both = jnp.concatenate(
            [in3[...].reshape(512, 128), twin_in[...].reshape(512, 128)], axis=1
        )
        spun = dot3((east[0], east[1]), split(both))
        spec_main[...] = spun[:512, :128] + sign512 * swap(spun[512:, :128])
        spec_twin[...] = spun[:512, 128:] + sign512 * swap(spun[512:, 128:])

    def second_step():
        arrived(xp.at[1 - core], RP2)
        arrived(xq.at[1 - core], RQ2)
        arrived(r2, R2)
        step0, p_val, resid = state["step0"], state["p_val"], state["resid"]
        g00, rr0 = state["g00"], state["rr0"]
        full_sum = jnp.sum(r2[...], axis=0)
        g11, g10 = unpack(full_sum, 0), unpack(full_sum, 1)
        rr1, r10 = unpack(full_sum, 2), unpack(full_sum, 3)
        beta = rr1 / rr0
        bent = (g11 + 2.0 * beta * g10 + beta * beta * g00) + damping[0] * (
            rr1 + 2.0 * beta * r10 + beta * beta * rr0
        )
        step1 = rr1 / bent
        coefs = step0 * p_val + step1 * (resid + beta * p_val)
        for m in range(4):
            coef_out[0, :, pl.ds(128 * m, 128)] = coefs[m:m + 1]
        state.update(alpha=step0 + step1 + step1 * beta, gamma=-step1 * step0)

    def shape_spectrum():
        copies[7].wait()
        copies[8].wait()
        copies[12].wait()
        alpha, gamma = state["alpha"], state["gamma"]
        rows_of = []
        extra = []
        for layer in range(2):
            coarse = alpha * xp[:, :, 8 * layer:8 * layer + 8, :].reshape(
                256, 256
            ) + gamma * xq[:, :, 8 * layer:8 * layer + 8, :].reshape(256, 256)
            north = dot3((north_hat[0], north_hat[1]), split(coarse))
            rows_of.append(north[:128])
            extra.append(north[128:144])
        rows_of.extend(extra)
        rows_of.append(jnp.zeros((96, 256), F32))
        model = dot3(
            (east_hat[0], east_hat[1]), split(jnp.concatenate(rows_of, axis=0)), transposed=True
        )
        left512 = lanes_of((512, 128)) < 64
        total = spec_main[...]
        twin = spec_twin[...]
        for layer in range(2):
            lanes = slice(128 * layer, 128 * layer + 128)
            plane = model[:512, lanes] - sign512 * swap(model[512:, lanes])
            total = total + filt[2 + layer] * plane
            top, bottom = model[:512, 256:], model[512:, 256:]
            if layer:
                top = pltpu.roll(top, 112, axis=1)
                bottom = pltpu.roll(bottom, 112, axis=1)
            twin = twin + filt[6 + layer] * jnp.where(left512, top, swap(bottom))
        shaped = filt[0] * total - filt[1] * swap(total)
        shaped_twin = filt[4] * twin - filt[5] * swap(twin)
        joined = special & (lanes_of((512, 128)) % 64 == 0)
        state["shaped"] = shaped - jnp.where(joined, sign512 * swap(shaped_twin), 0.0)

    def east_back():
        spun = dot3((east_inv[0], east_inv[1]), split(state["shaped"]))
        back = spun[:512] - sign512 * swap(spun[512:])
        sign16 = signs_of((16, 128))
        fine_c, fine_s = twist_fine[0, c], twist_fine[1, c]
        for mid in range(8):
            for top in range(4):
                base = 64 * mid + 16 * top
                block = back[base:base + 16]
                co = twist_coarse[8 * top + mid, c]
                si = twist_coarse[8 * top + mid, 8 + c]
                tc = co * fine_c - si * fine_s
                ts = si * fine_c + co * fine_s
                send4[mid, 16 * top:16 * top + 16, :] = block * tc - sign16 * ts * swap(block)
        cols_exchange(send4, in4, T3P)

    def east_last():
        arrived(in4, T3P)
        for pair in range(2):
            values = []
            for k in range(8):
                m0 = in4[k, 32 * pair:32 * pair + 16, :]
                m1 = in4[k, 32 * pair + 16:32 * pair + 32, :]
                values.append((jnp.where(left16, m0, swap(m1)), jnp.where(left16, swap(m0), m1)))
            for b, (re, im) in enumerate(short_transform(values, 1.0)):
                send5[4 * b + 2 * pair] = jnp.where(left16, re, swap(im))
                send5[4 * b + 2 * pair + 1] = jnp.where(left16, swap(re), im)
        rows_exchange(send5, in5, T3Q)

    def north_back():
        for i in range(9, 12):
            copies[i].wait()
        arrived(in5, T3Q)
        tw_c, tw_s = twist[0], twist[1]
        come = in5[...].reshape(16, 2, 16, 128)
        pair = jnp.concatenate(
            [come[:, 0].reshape(256, 128), come[:, 1].reshape(256, 128)], axis=1
        )
        pair_h, pair_l = split(pair)
        inner = dot3((pair_h, pair_l), (inner_inv[0], inner_inv[1]))
        first = dot3((pair_h[:16], pair_l[:16]), (first_inv[0], first_inv[1]))
        inner = jnp.concatenate([first, inner[16:]], axis=0)
        re, im = inner[:, :128].reshape(16, 16, 128), inner[:, 128:].reshape(16, 16, 128)
        turned = jnp.concatenate(
            [
                (re * tw_c - im * tw_s).reshape(256, 128),
                (im * tw_c + re * tw_s).reshape(256, 128),
            ],
            axis=0,
        )
        final = dot3((outer_inv[0], outer_inv[1]), split(turned))
        for i in range(32):
            map_out[:, pl.ds(128 * i, 128)] = final[16 * i:16 * i + 16]

    right_side()
    met()
    right_side_return()
    grid_rows()
    filter_tables()
    first_direction()
    first_image()
    north_forward()
    first_coarse()
    first_applied()
    first_sums()
    east_first()
    first_spread()
    second_image()
    second_coarse()
    first_step()
    second_sums()
    second_spread()
    east_second()
    second_step()
    shape_spectrum()
    east_back()
    east_last()
    north_back()

    for buf, phase in ((in1, T1), (send5, T3Q), (r1, R1), (r2, R2)):
        left(buf.at[pl.ds(0, ROWS - 1)], phase)
    for buf, phase in ((send2, T2A), (send4, T3P), (zp, ZP), (zq, ZQ), (z1, Z1), (z2, Z2)):
        left(buf.at[pl.ds(0, COLS - 1)], phase)

    for buf, phase, later in ((xp, RP, RP2), (xq, RQ, RQ2)):
        left(buf.at[0, pl.ds(0, ROWS // 2 - 1)], phase)
        left(buf.at[0], later)

    @pl.when(group == c)
    def _():
        left(send3.at[pl.ds(0, ROWS - 1)], T2B)

    @pl.when(group != c)
    def _():
        left(send3, T2B)

    @pl.when((c == 0) & (r == 0))
    def _():
        left(twin_send.at[pl.ds(0, 7)], TWIN)

    @pl.when((c == 0) & (r != 0))
    def _():
        left(twin_send, TWIN)

    halo_left(spread0.at[4], ret0, RETURN0, False)
    halo_left(p_own, halo0, COLLECT0, True)
    halo_left(spread1.at[4], ret1, RETURN1, False)
    halo_left(q_own, halo1, COLLECT1, True)


def settle(coef_in, map_in, coef_out, map_out):
    coef_out[...] = coef_in[...]
    map_out[...] = map_in[...]


def on_device(
    kernel_tiles, footprints, counts, readings, damping, layer_depth,
    inclinations, declinations, resid_grid,
):
    table = tables()
    consts = [jnp.asarray(table[name]) for name in TABLE_NAMES]
    shapes = [x.shape for x in consts]
    shapes[6] = shapes[6][1:]
    shapes[7] = shapes[7][1:]
    kinds = [x.dtype for x in consts]
    smem = pl.BlockSpec(memory_space=pltpu.SMEM)
    vmem = pl.BlockSpec(memory_space=pltpu.VMEM)
    hbm = pl.BlockSpec(memory_space=pl.ANY)

    def v(*shape):
        return pltpu.VMEM(shape, F32)

    block = (32, 16, 128)
    scratch = [v(9, 256, 512)]
    scratch += [pltpu.VMEM(shape, kind) for shape, kind in zip(shapes, kinds)]
    scratch += [
        v(*block), v(8, 32, 256), v(8, 32, 256), v(*block), v(*block),
        v(8, 16, 128), v(*block), v(8, 64, 128), v(8, 64, 128), v(*block), v(*block),
        v(512, 128), v(512, 128), v(8, 512, 128),
    ]
    scratch += [v(9, 8, 128) for _ in range(7)]
    scratch += [
        v(8, 128), v(8, 128), v(8, 8, 128), v(8, 8, 128),
        v(16, 256), v(16, 256), v(2, 16, 16, 256), v(2, 16, 16, 256),
        v(256, 128), v(256, 128), v(8, 128), v(8, 128), v(8, 128), v(8, 128),
        v(8, 8, 128), v(32, 8, 128), v(8, 8, 128), v(32, 8, 128),
    ]
    scratch += [
        pltpu.SemaphoreType.DMA((13,)),
        pltpu.SemaphoreType.DMA((PHASES,)),
        pltpu.SemaphoreType.DMA((PHASES,)),
        pltpu.SemaphoreType.DMA((4, 9)),
        pltpu.SemaphoreType.DMA((4, 9)),
    ]
    coef, rtp_map = pl.pallas_call(
        kernel,
        out_shape=(
            jax.ShapeDtypeStruct((1, 1, 512), F32),
            jax.ShapeDtypeStruct((16, FULL), F32),
        ),
        in_specs=[smem] * 7 + [hbm, vmem, vmem] + [hbm] * len(consts),
        out_specs=(vmem, vmem),
        scratch_shapes=scratch,
        compiler_params=pltpu.CompilerParams(
            collective_id=0, has_side_effects=True, vmem_limit_bytes=60 * 1024 * 1024
        ),
    )(
        footprints.reshape(9), counts.reshape(1), damping, layer_depth,
        inclinations, declinations,
        jnp.asarray(table["twist_coarse"]),
        kernel_tiles.reshape(9, 256, 512), readings.reshape(1, 256),
        resid_grid.reshape(block), *consts,
    )
    return pl.pallas_call(
        settle,
        out_shape=(
            jax.ShapeDtypeStruct((1, 1, 512), F32),
            jax.ShapeDtypeStruct((16, FULL), F32),
        ),
        in_specs=[vmem, vmem],
        out_specs=(vmem, vmem),
    )(coef, rtp_map)


def solution(mesh):
    in_specs = (
        P("row", "col", None, None, None),
        P("row", "col", None),
        P("row", "col"),
        P("row", "col", None),
        P(),
        P(),
        P(),
        P(),
        P("col", "row"),
    )
    out_specs = (P("row", "col", None), P(("row", "col"), None))
    return jax.shard_map(
        on_device, mesh=mesh, in_specs=in_specs, out_specs=out_specs, check_vma=False
    )
```

```python
import functools
import math

import jax
import jax.numpy as jnp
import ml_dtypes
import numpy as np
from jax import lax
from jax.experimental import pallas as pl
from jax.experimental.pallas import tpu as pltpu
from jax.sharding import PartitionSpec as P

F32 = jnp.float32
BF16 = jnp.bfloat16
MESH = pl.DeviceIdType.MESH
ROWS, COLS = 32, 8
FULL = 4096
REFINE = 16
SLOTS = 256
OFFSETS = tuple((a, b) for a in (-1, 0, 1) for b in (-1, 0, 1))
SCALE = 1.0 / 16777216.0

(T1, T2A, T2B, TWIN, T3P, T3Q, ZP, RP, ZQ, RQ, Z1, R1, Z2, R2, RP2, RQ2, T3P1, T3Q1) = range(18)
PHASES = 18
RETURN0, COLLECT0, RETURN1, COLLECT1 = range(4)


def halves(x):
    high = x.astype(np.float32).astype(ml_dtypes.bfloat16)
    low = (x - high.astype(np.float64)).astype(np.float32).astype(ml_dtypes.bfloat16)
    return np.stack([high, low])


@functools.lru_cache(maxsize=None)
def tables():
    two_pi = 2.0 * math.pi
    a = np.arange(32)
    ka = np.arange(16)
    n = np.arange(128)
    kn = np.arange(128)
    ang_a = two_pi * np.outer(ka, a) / 32
    outer = np.stack([np.cos(ang_a), -np.sin(ang_a)])
    outer[1, 0] = (-1.0) ** a
    eye = np.eye(16)
    outer_fwd = np.kron(outer.reshape(32, 32), eye)
    inv = np.stack([2 * np.cos(ang_a), -2 * np.sin(ang_a)])
    inv[0, 0] = 1.0
    inv[1, 0] = (-1.0) ** a
    outer_inv = np.kron(inv.reshape(32, 32).T, eye).reshape(512, 2, 16, 2, 8)
    outer_inv = outer_inv.transpose(0, 1, 3, 2, 4).reshape(512, 512)
    ang_t = two_pi * np.outer(ka, n) / 4096
    twist = np.stack([np.cos(ang_t), np.sin(ang_t)])[:, :, None, :]
    th = two_pi * np.outer(n, kn) / 128
    c, s = np.cos(th), np.sin(th)
    inner_fwd = np.block([[c, -s], [s, c]])
    inner_inv = np.block([[c.T, s.T], [-s.T, c.T]])
    k0 = np.arange(64)
    th0 = two_pi * np.outer(n, 32 * k0) / 4096
    th1 = two_pi * np.outer(n, 16 + 32 * k0) / 4096
    alt = (-1.0) ** n
    first_fwd = np.zeros((256, 256))
    first_fwd[:128, 0:64] = np.cos(th0)
    first_fwd[:128, 128:192] = -np.sin(th0)
    first_fwd[:128, 128] = alt
    first_fwd[128:, 64:128] = np.cos(th1)
    first_fwd[128:, 192:256] = -np.sin(th1)
    first_inv = np.zeros((256, 256))
    first_inv[0:64, :128] = 2 * np.cos(th0).T
    first_inv[0, :128] = 1.0
    first_inv[128:192, :128] = -2 * np.sin(th0).T
    first_inv[128, :128] = alt
    first_inv[64:128, 128:] = 2 * np.cos(th1).T
    first_inv[192:256, 128:] = -2 * np.sin(th1).T
    by_half = np.concatenate(
        [np.arange(64), 128 + np.arange(64), 64 + np.arange(64), 192 + np.arange(64)]
    )
    inner_inv, first_inv = inner_inv[by_half], first_inv[by_half]
    w = np.arange(512)
    th_w = two_pi * (np.outer(w, w) % 512) / 512
    east = np.concatenate([np.cos(th_w), np.sin(th_w)])
    back = np.arange(512).reshape(4, 8, 2, 8).transpose(2, 1, 0, 3).reshape(512)
    east_inv = np.concatenate([np.cos(th_w)[back], np.sin(th_w)[back]])
    kb = np.arange(8)
    ang_c = two_pi * np.outer(np.arange(32), 16 * kb) / 4096
    twist_coarse = np.concatenate([np.cos(ang_c), np.sin(ang_c)], axis=1)
    ang_f = two_pi * np.outer(kb, np.arange(16)) / 4096
    twist_fine = np.broadcast_to(
        np.stack([np.cos(ang_f), np.sin(ang_f)])[..., None], (2, 8, 16, 128)
    )
    u = np.arange(4096)
    g = np.arange(256)
    hat = np.maximum(0.0, 1.0 - np.abs((u[:, None] + 0.5) / REFINE - 0.5 - g[None, :]))
    spec = np.fft.fft(hat, axis=0)
    east_hat = np.stack(
        [np.concatenate([spec[k::8].real, spec[k::8].imag]) for k in range(8)]
    )
    order = np.array(
        [
            8 * (2 * chip + core) + 4 * m2 + g4
            for core in range(2) for chip in range(16) for g4 in range(4) for m2 in range(2)
        ]
    )
    north_hat = np.zeros((32, 144, 256))
    lane = np.arange(64)
    for col in range(8):
        for ka1 in range(2):
            for knh in range(2):
                slot = 2 * col + ka1
                ku = slot + 32 * (64 * knh + lane) if slot else 16 * knh + 32 * lane
                idx = col * 4 + ka1 * 2 + knh
                north_hat[idx, :64] = spec[ku].real[:, order]
                north_hat[idx, 64:128] = spec[ku].imag[:, order]
    north_hat[0, 128] = spec[2048].real[order]
    f32 = np.float32
    return dict(
        outer_fwd=halves(outer_fwd),
        outer_inv=halves(outer_inv),
        inner_fwd=halves(inner_fwd),
        inner_inv=halves(inner_inv),
        first_fwd=halves(first_fwd),
        first_inv=halves(first_inv),
        east=halves(east),
        east_inv=halves(east_inv),
        twist=twist.astype(f32),
        twist_fine=np.ascontiguousarray(twist_fine).astype(f32),
        twist_coarse=twist_coarse.astype(f32),
        east_hat=np.ascontiguousarray(halves(east_hat).swapaxes(0, 1)),
        north_hat=np.ascontiguousarray(halves(north_hat).swapaxes(0, 1)),
    )


TABLE_NAMES = (
    "outer_fwd",
    "inner_fwd",
    "first_fwd",
    "twist",
    "twist_fine",
    "east",
    "north_hat",
    "east_hat",
    "inner_inv",
    "first_inv",
    "outer_inv",
    "east_inv",
)


def split(x):
    high = x.astype(BF16)
    return high, (x - high.astype(F32)).astype(BF16)


def dot3(lhs, rhs, transposed=False):
    dims = (((1,), (1 if transposed else 0,)), ((), ()))

    def one(x, y):
        return lax.dot_general(x, y, dims, preferred_element_type=F32)

    return one(lhs[0], rhs[0]) + (one(lhs[0], rhs[1]) + one(lhs[1], rhs[0]))


def short_transform(values, sign):
    count = len(values)
    if count == 1:
        return values
    even = short_transform(values[0::2], sign)
    odd = short_transform(values[1::2], sign)
    out = [None] * count
    for k in range(count // 2):
        re, im = odd[k]
        if k == 0:
            pass
        elif 4 * k == count:
            re, im = -sign * im, sign * re
        else:
            co = math.cos(2 * math.pi * k / count)
            si = sign * math.sin(2 * math.pi * k / count)
            re, im = re * co - im * si, re * si + im * co
        ere, eim = even[k]
        out[k] = (ere + re, eim + im)
        out[k + count // 2] = (ere - re, eim - im)
    return out


def pole_of(fn, fe, angles):
    radius = jnp.sqrt(fn * fn + fe * fe)
    safe = jnp.where(radius > 0.0, radius, 1.0)
    nn = jnp.where(radius > 0.0, fn / safe, 0.0)
    ne = jnp.where(radius > 0.0, fe / safe, 0.0)
    re = im = None
    for m in range(2):
        vertical = angles[m]
        horizontal = angles[2 + m]
        along = horizontal * (angles[4 + m] * nn + angles[6 + m] * ne)
        inverse = 1.0 / (vertical * vertical + along * along)
        one_re, one_im = vertical * inverse, -along * inverse
        if re is None:
            re, im = one_re, one_im
        else:
            re, im = re * one_re - im * one_im, re * one_im + im * one_re
    return re, im, radius


def lanes_of(shape):
    return lax.broadcasted_iota(jnp.int32, shape, len(shape) - 1)


def signs_of(shape):
    return jnp.where(lanes_of(shape) < 64, 1.0, -1.0).astype(F32)


def swap(x):
    return pltpu.roll(x, 64, axis=x.ndim - 1)


def kernel(
    foot, counts, damping, depth, inclinations, declinations, twist_coarse,
    tiles_hbm, readings, grid,
    outer_fwd_h, inner_fwd_h, first_fwd_h, twist_h, twist_fine_h, east_h,
    north_hat_h, east_hat_h, inner_inv_h, first_inv_h, outer_inv_h,
    east_inv_h,
    coef_out, map_out,
    tiles, outer_fwd, inner_fwd, first_fwd, twist, twist_fine, east,
    north_hat, east_hat, inner_inv, first_inv, outer_inv,
    east_inv,
    in1, send2, in2, send3, in3, twin_send, twin_in, send4, in4, send5, in5,
    spec_main, spec_twin, filt,
    spread0, spread1, in_order, ret0, ret1, halo0, halo1, chosen,
    p_own, q_own, zp, zq, xp_send, xq_send, xp, xq,
    y_p, y_q, sum1, sum2, sum1b, sum2b, z1, r1, z2, r2,
    tile_sem, load_sem, send_sem, recv_sem, halo_send, halo_recv,
):
    r = lax.axis_index("row")
    c = lax.axis_index("col")
    group = r // 4
    low2 = r % 4
    special = r == 0

    loads = [
        (outer_fwd_h, outer_fwd),
        (inner_fwd_h, inner_fwd),
        (first_fwd_h, first_fwd),
        (twist_h, twist),
        (twist_fine_h, twist_fine),
        (east_h, east),
        (north_hat_h.at[r], north_hat),
        (east_hat_h.at[c], east_hat),
        (inner_inv_h, inner_inv),
        (first_inv_h, first_inv),
        (outer_inv_h, outer_inv),
        (east_inv_h, east_inv),
    ]
    copies = [
        pltpu.make_async_copy(src, dst, load_sem.at[i]) for i, (src, dst) in enumerate(loads)
    ]

    def tile_copy(k):
        return pltpu.make_async_copy(tiles_hbm.at[k], tiles.at[k], tile_sem.at[k])

    for k in range(9):
        tile_copy(k).start()

    core = r % 2
    chip = r // 2
    cols_far = [(c + step) % COLS for step in (4, 3, 5, 2, 6, 1, 7)]
    along_x = [8 * ((r // 8 + step) % 4) for step in (2, 1, 3, 0)]
    along_y = [2 * ((chip + step) % 4) for step in (2, 1, 3, 0)]
    rows_far = [x + y + one for x in along_x for y in along_y for one in (1 - core, core)][:-1]

    barrier = pltpu.get_barrier_semaphore()

    def greet(row, col):
        pl.semaphore_signal(barrier, inc=1, device_id=(row, col), device_id_type=MESH)

    def exists(a, b):
        return (r + a >= 0) & (r + a < ROWS) & (c + b >= 0) & (c + b < COLS)

    for row in rows_far:
        greet(row, c)
    for col in cols_far:
        greet(r, col)

    expected = jnp.int32(ROWS - 1 + COLS - 1)
    for a in (-1, 1):
        for b in (-1, 1):
            there = exists(a, b)
            expected = expected + there.astype(jnp.int32)

            @pl.when(there)
            def _():
                greet(r + a, c + b)

    def push(src, dst, phase, row, col):
        pltpu.make_async_remote_copy(
            src_ref=src, dst_ref=dst, send_sem=send_sem.at[phase], recv_sem=recv_sem.at[phase],
            device_id=(row, col), device_id_type=MESH,
        ).start()

    def keep(src, dst, phase):
        pltpu.make_async_copy(src, dst, recv_sem.at[phase]).start()

    def arrived(dst, phase):
        pltpu.make_async_copy(dst, dst, recv_sem.at[phase]).wait()

    def left(ref, phase):
        pltpu.make_async_copy(ref, ref, send_sem.at[phase]).wait()

    def rows_exchange(src, dst, phase):
        keep(src.at[r], dst.at[r], phase)

        for row in rows_far:
            push(src.at[row], dst.at[r], phase, row, c)

    def cols_exchange(src, dst, phase):
        keep(src.at[c], dst.at[c], phase)

        for col in cols_far:
            push(src.at[col], dst.at[c], phase, r, col)

    def rows_share(src, dst, phase):
        keep(src, dst.at[r], phase)
        for row in rows_far:
            push(src, dst.at[r], phase, row, c)

    def chips_share(src, dst, phase):
        keep(src, dst.at[core, chip], phase)

        for row in rows_far[1::2]:
            push(src, dst.at[core, chip], phase, row, c)

    def chip_share(dst, phase_in, phase_out):
        arrived(dst.at[core], phase_in)
        push(dst.at[core], dst.at[core], phase_out, r + 1 - 2 * core, c)

    def cols_share(src, dst, phase):
        keep(src, dst.at[c], phase)

        for col in cols_far:
            push(src, dst.at[c], phase, r, col)

    def halo_copy(src, dst, turn, code, row, col):
        return pltpu.make_async_remote_copy(
            src_ref=src, dst_ref=dst,
            send_sem=halo_send.at[turn, code], recv_sem=halo_recv.at[turn, code],
            device_id=(row, col), device_id_type=MESH,
        )

    def return_start(spread, dst, turn):
        for code, (a, b) in enumerate(OFFSETS):
            if code != 4:

                @pl.when(exists(a, b))
                def _():
                    halo_copy(spread.at[code], dst.at[code], turn, code, r + a, c + b).start()

    def collect_start(own, dst, turn):
        for code, (a, b) in enumerate(OFFSETS):
            if code != 4:

                @pl.when(exists(-a, -b))
                def _():
                    halo_copy(own, dst.at[code], turn, code, r - a, c - b).start()

    def halo_wait(src, dst, turn, collecting):
        for code, (a, b) in enumerate(OFFSETS):
            if code != 4:
                away = -1 if collecting else 1
                source = exists(-away * a, -away * b)

                @pl.when(source)
                def _():
                    halo_copy(src, dst.at[code], turn, code, r, c).wait_recv()

                @pl.when(jnp.logical_not(source))
                def _():
                    dst[code] = jnp.zeros((8, 128), F32)

    def halo_left(src, dst, turn, collecting):
        for code, (a, b) in enumerate(OFFSETS):
            if code != 4:
                away = -1 if collecting else 1

                @pl.when(exists(away * a, away * b))
                def _():
                    halo_copy(src, dst.at[code], turn, code, r, c).wait_send()

    sub8 = lax.broadcasted_iota(jnp.int32, (8, 128), 0)

    def place_of(code):
        k = jnp.int32(0)
        for j in range(9):
            k = jnp.where(foot[j] == code, j, k)
        return k

    def block_of(k, y):
        total = jnp.zeros((8, 128), F32)
        for m in range(4):
            acc = [jnp.zeros((8, 128), F32) for _ in range(4)]
            for t in range(32):
                part = tiles[k, pl.ds(8 * t, 8), pl.ds(128 * m, 128)]
                acc[t % 4] = acc[t % 4] + part * y[pl.ds(8 * t, 8), :]
            row = jnp.sum((acc[0] + acc[1]) + (acc[2] + acc[3]), axis=0, keepdims=True)
            total = total + jnp.where(sub8 == m, jnp.broadcast_to(row, (8, 128)), 0.0)
        return total

    def spread_of(y, out):
        @pl.loop(0, 9)
        def _(code):
            out[code] = block_of(place_of(code), y)

    def readings_of(blocks, y):
        @pl.loop(0, 8)
        def _(chunk):
            base = pl.multiple_of(32 * chunk, 32)
            acc = [jnp.zeros((8, 128), F32) for _ in range(4)]
            for k in range(9):
                code = foot[k]
                for m in range(4):
                    row = jnp.broadcast_to(blocks[code, pl.ds(m, 1), :], (8, 128))
                    for t in range(4):
                        part = tiles[k, pl.ds(base + 8 * t, 8), pl.ds(128 * m, 128)]
                        acc[t] = acc[t] + part * row
            for t in range(4):
                slot = lax.broadcasted_iota(jnp.int32, (8, 128), 0) + (base + 8 * t)
                total = jnp.sum(acc[t], axis=1, keepdims=True)
                y[pl.ds(base + 8 * t, 8), :] = jnp.where(
                    slot < counts[0], jnp.broadcast_to(total, (8, 128)), 0.0
                )

    def gather_blocks(own, halo):
        for code in range(9):
            chosen[code] = own[...] if code == 4 else halo[code]

    def own_sum(spread, ret):
        total = spread[4]
        for code in range(9):
            if code != 4:
                total = total + ret[code]
        return total

    def total_of(x):
        return jnp.sum(jnp.sum(x, axis=1, keepdims=True), axis=0, keepdims=True)

    lane8 = lanes_of((8, 128))

    lane1 = lanes_of((1, 128))

    def pack(parts):
        out = jnp.zeros((1, 128), F32)
        for i, part in enumerate(parts):
            out = jnp.where(lane1 == i, jnp.broadcast_to(part, (1, 128)), out)
        return out

    def unpack(x, i):
        return jnp.sum(jnp.where(lane1 == i, x, 0.0), axis=1, keepdims=True)

    state = {}
    sign512 = signs_of((512, 128))
    left16 = lanes_of((16, 128)) < 64

    def met():
        pl.semaphore_wait(barrier, expected)

    def grid_rows():
        rows_exchange(grid, in1, T1)

    def right_side():
        eye = lax.broadcasted_iota(jnp.int32, (SLOTS, SLOTS), 0) == lanes_of((SLOTS, SLOTS))
        column = jnp.sum(
            jnp.where(eye, jnp.broadcast_to(readings[...], (SLOTS, SLOTS)), 0.0),
            axis=1, keepdims=True,
        )
        slot_index = lax.broadcasted_iota(jnp.int32, (SLOTS, 128), 0)
        y_q[...] = jnp.where(
            slot_index < counts[0], jnp.broadcast_to(column, (SLOTS, 128)), 0.0
        )
        for one in copies:
            one.start()

        @pl.loop(0, 9)
        def _(k):
            tile_copy(k).wait()
            in_order[k] = block_of(k, y_q)

        @pl.loop(0, 9)
        def _(code):
            spread0[code] = in_order[place_of(code)]

    def right_side_return():
        return_start(spread0, ret0, RETURN0)

    def north_forward():
        for i in range(0, 3):
            copies[i].wait()
        copies[3].wait()
        arrived(in1, T1)
        outer = dot3(
            (outer_fwd[0], outer_fwd[1]), split(in1[...].reshape(512, 128))
        ).reshape(2, 16, 16, 128)
        tw_c, tw_s = twist[0], twist[1]
        turned = jnp.concatenate(
            [
                (outer[0] * tw_c + outer[1] * tw_s).reshape(256, 128),
                (outer[1] * tw_c - outer[0] * tw_s).reshape(256, 128),
            ],
            axis=1,
        )
        turned_h, turned_l = split(turned)
        send2[...] = dot3((turned_h, turned_l), (inner_fwd[0], inner_fwd[1])).reshape(8, 32, 256)
        send2[0, 0:16, :] = dot3((turned_h[:16], turned_l[:16]), (first_fwd[0], first_fwd[1]))
        cols_exchange(send2, in2, T2A)

    def first_direction():
        halo_wait(spread0.at[4], ret0, RETURN0, False)
        p_own[...] = own_sum(spread0, ret0)
        collect_start(p_own, halo0, COLLECT0)
        cols_share(p_own, zp, ZP)

    def first_image():
        halo_wait(p_own, halo0, COLLECT0, True)
        gather_blocks(p_own, halo0)
        readings_of(chosen, y_p)
        p_val = p_own[...]
        sum1[...] = pack([total_of(y_p[...] * y_p[...]) * (1.0 / 128.0), total_of(p_val * p_val)])
        cols_share(sum1, z1, Z1)
        spread_of(y_p, spread1)
        return_start(spread1, ret1, RETURN1)

    lane_half = lanes_of((8, 128)) // 32

    def coarse_rows(z, out):
        for half in range(2):
            for g in range(4):
                total = jnp.zeros((8, 128), F32)
                for j in range(4):
                    block = z[4 * half + j]
                    shift = (32 * (j - g)) % 128
                    if shift:
                        block = pltpu.roll(block, shift, axis=1)
                    total = jnp.where(lane_half == j, block, total)
                lanes = pl.ds(128 * half, 128)
                out[pl.ds(2 * g, 2), lanes] = total[0:2]
                out[pl.ds(8 + 2 * g, 2), lanes] = total[2:4]

    def first_coarse():
        arrived(zp, ZP)
        coarse_rows(zp, xp_send)
        chips_share(xp_send, xp, RP)

    def east_first():
        copies[4].wait()
        arrived(in2, T2A)
        pairs = short_transform(
            [(in2[b, :, 0:128], in2[b, :, 128:256]) for b in range(8)], -1.0
        )
        lane32 = lanes_of((32, 128))
        sub32 = lax.broadcasted_iota(jnp.int32, (32, 128), 0)
        apart = (lane32 == 0) & (sub32 < 16) & (c == 0)
        for k in range(8):
            re, im = pairs[k]
            other_re, other_im = pairs[(8 - k) % 8]
            main_re = jnp.where(apart, 0.5 * (re + other_re), re)
            main_im = jnp.where(apart, 0.5 * (im - other_im), im)
            twin_re = 0.5 * (im[:16] + other_im[:16])
            twin_im = 0.5 * (other_re[:16] - re[:16])
            co = twist_coarse[r, k]
            si = twist_coarse[r, 8 + k]
            fine_c, fine_s = twist_fine[0, k], twist_fine[1, k]
            tc = co * fine_c - si * fine_s
            ts = si * fine_c + co * fine_s
            for ka1 in range(2):
                xr, xi = main_re[16 * ka1:16 * ka1 + 16], main_im[16 * ka1:16 * ka1 + 16]
                yr, yi = xr * tc + xi * ts, xi * tc - xr * ts
                send3[4 * k + 2 * ka1] = jnp.where(left16, yr, swap(yi))
                send3[4 * k + 2 * ka1 + 1] = jnp.where(left16, swap(yr), yi)
            yr, yi = twin_re * tc + twin_im * ts, twin_im * tc - twin_re * ts
            twin_send[k] = jnp.where(left16, yr, swap(yi))
        mine = group == c

        @pl.loop(0, ROWS)
        def _(i):
            half = (i // 4 + 1) // 2
            k = (c + jnp.where(i // 4 % 2 == 1, 4 - half, 4 + half)) % COLS
            low = (low2 + i) % 4
            block = send3.at[4 * k + low]

            @pl.when(mine & (k == c) & (low == low2))
            def _():
                keep(block, in3.at[r], T2B)

            @pl.when(jnp.logical_not(mine & (k == c) & (low == low2)))
            def _():
                push(block, in3.at[r], T2B, 4 * c + low, k)

        @pl.when(c == 0)
        def _():
            @pl.loop(0, COLS)
            def _(k):
                @pl.when((k == 0) & (r == 0))
                def _():
                    keep(twin_send.at[k], twin_in.at[r], TWIN)

                @pl.when(jnp.logical_not((k == 0) & (r == 0)))
                def _():
                    push(twin_send.at[k], twin_in.at[r], TWIN, 0, k)

    def sum_of(x, count):
        total = x[0]
        for i in range(1, count):
            total = total + x[i]
        return total

    def share_sums(z, mine, out, phase_in, phase_out):
        arrived(z, phase_in)
        mine[...] = sum_of(z, COLS)
        rows_share(mine, out, phase_out)

    def first_applied():
        halo_wait(spread1.at[4], ret1, RETURN1, False)
        q_own[...] = own_sum(spread1, ret1) + damping[0] * p_own[...]
        collect_start(q_own, halo1, COLLECT1)
        cols_share(q_own, zq, ZQ)

    def first_spread():
        chip_share(xp, RP, RP2)

    def second_spread():
        chip_share(xq, RQ, RQ2)

    def first_sums():
        share_sums(z1, sum1b, r1, Z1, R1)

    def second_image():
        halo_wait(q_own, halo1, COLLECT1, True)
        gather_blocks(q_own, halo1)
        readings_of(chosen, y_q)

    def second_coarse():
        arrived(zq, ZQ)
        coarse_rows(zq, xq_send)
        chips_share(xq_send, xq, RQ)

    def first_step():
        arrived(r1, R1)
        weight = damping[0]
        full_sum = jnp.sum(r1[...], axis=0)
        g00, rr0 = unpack(full_sum, 0), unpack(full_sum, 1)
        step0 = rr0 / (g00 + weight * rr0)
        p_val = p_own[...]
        resid = p_val - step0 * q_own[...]
        yr1 = y_p[...] - step0 * y_q[...]
        sum2[...] = pack(
            [
                total_of(yr1 * yr1) * (1.0 / 128.0),
                total_of(yr1 * y_p[...]) * (1.0 / 128.0),
                total_of(resid * resid),
                total_of(resid * p_val),
            ]
        )
        cols_share(sum2, z2, Z2)
        state.update(step0=step0, p_val=p_val, resid=resid, g00=g00, rr0=rr0)

    def second_sums():
        share_sums(z2, sum2b, r2, Z2, R2)

    def filter_tables():
        knh = low2 % 2
        ka = 2 * group + low2 // 2
        given = [inclinations[0], inclinations[1], declinations[0], declinations[1]]
        spot = jnp.zeros((8, 128), F32)
        for i, one in enumerate(given):
            spot = jnp.where(lane8 == i, one, spot)
        sines, cosines = jnp.sin(spot), jnp.cos(spot)

        def taken(x, i):
            return jnp.max(jnp.where(lane8 == i, x, -2.0)[0:1], axis=1, keepdims=True)

        angles = [taken(sines, 0), taken(sines, 1), taken(cosines, 0), taken(cosines, 1)]
        angles += [taken(cosines, 2), taken(cosines, 3), taken(sines, 2), taken(sines, 3)]

        @pl.loop(0, 16)
        def _(chunk):
            base = pl.multiple_of(32 * chunk, 32)
            shape = (32, 128)
            lane = lanes_of(shape)
            kv = c + 8 * (lax.broadcasted_iota(jnp.int32, shape, 0) + base)
            ku = jnp.where(ka > 0, ka + 32 * (64 * knh + lane), 16 * knh + 32 * lane)
            ku = jnp.where(lane < 64, ku, 2048)
            fe = jnp.where(kv < 2048, kv, kv - 4096).astype(F32) * (1.0 / 4096.0)
            fn = jnp.where(ku < 2048, ku, ku - 4096).astype(F32) * (1.0 / 4096.0)
            re_a, im_a, radius = pole_of(fn, fe, angles)
            re_b, im_b, _ = pole_of(
                jnp.where(ku == 2048, 0.5, fn), jnp.where(kv == 2048, 0.5, fe), angles
            )
            kappa = (2.0 * math.pi) * radius
            made = [
                (0.5 * SCALE) * (re_a + re_b),
                (0.5 * SCALE) * (im_a + im_b),
                jnp.exp(-kappa * depth[0]),
                jnp.exp(-kappa * depth[1]),
            ]
            for i, one in enumerate(made):
                other = swap(one)
                main = jnp.where(lane < 64, one, other)
                twin = jnp.where(lane < 64, other, one)
                if i == 1:
                    sign = signs_of(shape)
                    main, twin = main * sign, twin * sign
                filt[i, pl.ds(base, 32), :] = main
                filt[4 + i, pl.ds(base, 32), :] = twin

    def east_second():
        copies[5].wait()
        arrived(in3, T2B)

        @pl.when(special)
        def _():
            arrived(twin_in, TWIN)

        @pl.when(jnp.logical_not(special))
        def _():
            twin_in[...] = jnp.zeros((32, 16, 128), F32)

        both = jnp.concatenate(
            [in3[...].reshape(512, 128), twin_in[...].reshape(512, 128)], axis=1
        )
        spun = dot3((east[0], east[1]), split(both))
        spec_main[...] = spun[:512, :128] + sign512 * swap(spun[512:, :128])
        spec_twin[...] = spun[:512, 128:] + sign512 * swap(spun[512:, 128:])

    def second_step():
        arrived(xp.at[1 - core], RP2)
        arrived(xq.at[1 - core], RQ2)
        arrived(r2, R2)
        step0, p_val, resid = state["step0"], state["p_val"], state["resid"]
        g00, rr0 = state["g00"], state["rr0"]
        full_sum = jnp.sum(r2[...], axis=0)
        g11, g10 = unpack(full_sum, 0), unpack(full_sum, 1)
        rr1, r10 = unpack(full_sum, 2), unpack(full_sum, 3)
        beta = rr1 / rr0
        bent = (g11 + 2.0 * beta * g10 + beta * beta * g00) + damping[0] * (
            rr1 + 2.0 * beta * r10 + beta * beta * rr0
        )
        step1 = rr1 / bent
        coefs = step0 * p_val + step1 * (resid + beta * p_val)
        for m in range(4):
            coef_out[0, :, pl.ds(128 * m, 128)] = coefs[m:m + 1]
        state.update(alpha=step0 + step1 + step1 * beta, gamma=-step1 * step0)

    def shape_spectrum():
        copies[6].wait()
        copies[7].wait()
        copies[11].wait()
        alpha, gamma = state["alpha"], state["gamma"]
        rows_of = []
        extra = []
        for layer in range(2):
            coarse = alpha * xp[:, :, 8 * layer:8 * layer + 8, :].reshape(
                256, 256
            ) + gamma * xq[:, :, 8 * layer:8 * layer + 8, :].reshape(256, 256)
            north = dot3((north_hat[0], north_hat[1]), split(coarse))
            rows_of.append(north[:128])
            extra.append(north[128:144])
        rows_of.extend(extra)
        rows_of.append(jnp.zeros((96, 256), F32))
        model = dot3(
            (east_hat[0], east_hat[1]), split(jnp.concatenate(rows_of, axis=0)), transposed=True
        )
        left512 = lanes_of((512, 128)) < 64
        total = spec_main[...]
        twin = spec_twin[...]
        for layer in range(2):
            lanes = slice(128 * layer, 128 * layer + 128)
            plane = model[:512, lanes] - sign512 * swap(model[512:, lanes])
            total = total + filt[2 + layer] * plane
            top, bottom = model[:512, 256:], model[512:, 256:]
            if layer:
                top = pltpu.roll(top, 112, axis=1)
                bottom = pltpu.roll(bottom, 112, axis=1)
            twin = twin + filt[6 + layer] * jnp.where(left512, top, swap(bottom))
        shaped = filt[0] * total - filt[1] * swap(total)
        shaped_twin = filt[4] * twin - filt[5] * swap(twin)
        joined = special & (lanes_of((512, 128)) % 64 == 0)
        state["shaped"] = shaped - jnp.where(joined, sign512 * swap(shaped_twin), 0.0)

    def east_back():
        spun = dot3((east_inv[0], east_inv[1]), split(state["shaped"]))
        back = spun[:512] - sign512 * swap(spun[512:])
        sign8 = signs_of((8, 128))
        for half in range(2):
            rows = slice(8 * half, 8 * half + 8)
            fine_c, fine_s = twist_fine[0, c, rows, :], twist_fine[1, c, rows, :]
            for mid in range(8):
                for top in range(4):
                    base = 256 * half + 32 * mid + 8 * top
                    block = back[base:base + 8]
                    co = twist_coarse[8 * top + mid, c]
                    si = twist_coarse[8 * top + mid, 8 + c]
                    tc = co * fine_c - si * fine_s
                    ts = si * fine_c + co * fine_s
                    send4[half, mid, 8 * top:8 * top + 8, :] = (
                        block * tc - sign8 * ts * swap(block)
                    )
            cols_exchange(send4.at[half], in4.at[half], (T3P, T3P1)[half])

    def east_last():
        left8 = lanes_of((8, 128)) < 64
        for half in range(2):
            arrived(in4.at[half], (T3P, T3P1)[half])
            for pair in range(2):
                values = []
                for k in range(8):
                    m0 = in4[half, k, 16 * pair:16 * pair + 8, :]
                    m1 = in4[half, k, 16 * pair + 8:16 * pair + 16, :]
                    values.append(
                        (jnp.where(left8, m0, swap(m1)), jnp.where(left8, swap(m0), m1))
                    )
                for b, (re, im) in enumerate(short_transform(values, 1.0)):
                    send5[half, 4 * b + 2 * pair] = jnp.where(left8, re, swap(im))
                    send5[half, 4 * b + 2 * pair + 1] = jnp.where(left8, swap(re), im)
            rows_exchange(send5.at[half], in5.at[half], (T3Q, T3Q1)[half])

    def north_back():
        for i in range(8, 11):
            copies[i].wait()
        arrived(in5.at[0], T3Q)
        arrived(in5.at[1], T3Q1)
        tw_c, tw_s = twist[0], twist[1]
        come = in5[...].reshape(2, 16, 2, 8, 128)
        pair = jnp.concatenate(
            [come[:, :, 0].reshape(256, 128), come[:, :, 1].reshape(256, 128)], axis=1
        )
        inner = dot3(split(pair), (inner_inv[0], inner_inv[1]))
        lead = jnp.concatenate([pair[0:8], pair[128:136]], axis=0)
        first = dot3(split(lead), (first_inv[0], first_inv[1]))
        inner = jnp.concatenate(
            [first[:8], inner[8:128], first[8:], inner[136:]], axis=0
        )
        re = inner[:, :128].reshape(2, 16, 8, 128)
        im = inner[:, 128:].reshape(2, 16, 8, 128)
        turned = jnp.concatenate(
            [
                (re * tw_c - im * tw_s).reshape(256, 128),
                (im * tw_c + re * tw_s).reshape(256, 128),
            ],
            axis=0,
        )
        final = dot3((outer_inv[0], outer_inv[1]), split(turned))
        for i in range(32):
            map_out[:, pl.ds(128 * i, 128)] = final[16 * i:16 * i + 16]

    right_side()
    met()
    right_side_return()
    grid_rows()
    filter_tables()
    first_direction()
    first_image()
    north_forward()
    first_coarse()
    first_applied()
    first_sums()
    east_first()
    first_spread()
    second_image()
    second_coarse()
    first_step()
    second_sums()
    second_spread()
    east_second()
    second_step()
    shape_spectrum()
    east_back()
    east_last()
    north_back()
    for buf, phase in ((in1, T1), (send5.at[0], T3Q), (send5.at[1], T3Q1), (r1, R1), (r2, R2)):
        left(buf.at[pl.ds(0, ROWS - 1)], phase)
    for buf, phase in ((send2, T2A), (send4.at[0], T3P), (send4.at[1], T3P1), (zp, ZP), (zq, ZQ), (z1, Z1), (z2, Z2)):
        left(buf.at[pl.ds(0, COLS - 1)], phase)

    for buf, phase, later in ((xp, RP, RP2), (xq, RQ, RQ2)):
        left(buf.at[0, pl.ds(0, ROWS // 2 - 1)], phase)
        left(buf.at[0], later)

    @pl.when(group == c)
    def _():
        left(send3.at[pl.ds(0, ROWS - 1)], T2B)

    @pl.when(group != c)
    def _():
        left(send3, T2B)

    @pl.when((c == 0) & (r == 0))
    def _():
        left(twin_send.at[pl.ds(0, 7)], TWIN)

    @pl.when((c == 0) & (r != 0))
    def _():
        left(twin_send, TWIN)

    halo_left(spread0.at[4], ret0, RETURN0, False)
    halo_left(p_own, halo0, COLLECT0, True)
    halo_left(spread1.at[4], ret1, RETURN1, False)
    halo_left(q_own, halo1, COLLECT1, True)


def settle(coef_in, map_in, coef_out, map_out):
    coef_out[...] = coef_in[...]
    map_out[...] = map_in[...]


def on_device(
    kernel_tiles, footprints, counts, readings, damping, layer_depth,
    inclinations, declinations, resid_grid,
):
    table = tables()
    consts = [jnp.asarray(table[name]) for name in TABLE_NAMES]
    shapes = [x.shape for x in consts]
    shapes[6] = shapes[6][1:]
    shapes[7] = shapes[7][1:]
    kinds = [x.dtype for x in consts]
    smem = pl.BlockSpec(memory_space=pltpu.SMEM)
    vmem = pl.BlockSpec(memory_space=pltpu.VMEM)
    hbm = pl.BlockSpec(memory_space=pl.ANY)

    def v(*shape):
        return pltpu.VMEM(shape, F32)

    block = (32, 16, 128)
    scratch = [v(9, 256, 512)]
    scratch += [pltpu.VMEM(shape, kind) for shape, kind in zip(shapes, kinds)]
    scratch += [
        v(*block), v(8, 32, 256), v(8, 32, 256), v(*block), v(*block),
        v(8, 16, 128), v(*block), v(2, 8, 32, 128), v(2, 8, 32, 128),
        v(2, 32, 8, 128), v(2, 32, 8, 128),
        v(512, 128), v(512, 128), v(8, 512, 128),
    ]
    scratch += [v(9, 8, 128) for _ in range(8)]
    scratch += [
        v(8, 128), v(8, 128), v(8, 8, 128), v(8, 8, 128),
        v(16, 256), v(16, 256), v(2, 16, 16, 256), v(2, 16, 16, 256),
        v(256, 128), v(256, 128), v(1, 128), v(1, 128), v(1, 128), v(1, 128),
        v(8, 1, 128), v(32, 1, 128), v(8, 1, 128), v(32, 1, 128),
    ]
    scratch += [
        pltpu.SemaphoreType.DMA((9,)),
        pltpu.SemaphoreType.DMA((12,)),
        pltpu.SemaphoreType.DMA((PHASES,)),
        pltpu.SemaphoreType.DMA((PHASES,)),
        pltpu.SemaphoreType.DMA((4, 9)),
        pltpu.SemaphoreType.DMA((4, 9)),
    ]
    coef, rtp_map = pl.pallas_call(
        kernel,
        out_shape=(
            jax.ShapeDtypeStruct((1, 1, 512), F32),
            jax.ShapeDtypeStruct((16, FULL), F32),
        ),
        in_specs=[smem] * 7 + [hbm, vmem, vmem] + [hbm] * len(consts),
        out_specs=(vmem, vmem),
        scratch_shapes=scratch,
        compiler_params=pltpu.CompilerParams(
            collective_id=0, has_side_effects=True, vmem_limit_bytes=60 * 1024 * 1024
        ),
    )(
        footprints.reshape(9), counts.reshape(1), damping, layer_depth,
        inclinations, declinations,
        jnp.asarray(table["twist_coarse"]),
        kernel_tiles.reshape(9, 256, 512), readings.reshape(1, 256),
        resid_grid.reshape(block), *consts,
    )
    return pl.pallas_call(
        settle,
        out_shape=(
            jax.ShapeDtypeStruct((1, 1, 512), F32),
            jax.ShapeDtypeStruct((16, FULL), F32),
        ),
        in_specs=[vmem, vmem],
        out_specs=(vmem, vmem),
    )(coef, rtp_map)


def solution(mesh):
    in_specs = (
        P("row", "col", None, None, None),
        P("row", "col", None),
        P("row", "col"),
        P("row", "col", None),
        P(),
        P(),
        P(),
        P(),
        P("col", "row"),
    )
    out_specs = (P("row", "col", None), P(("row", "col"), None))
    return jax.shard_map(
        on_device, mesh=mesh, in_specs=in_specs, out_specs=out_specs, check_vma=False
    )
```
